512 devices in a mesh: dp: 8 (over y), expert: 64 (over x, z, core).
Axes of the slice: x: 4, y: 8, z: 8, core: 2. Of those that a mesh axis runs over, the one named last changes fastest.
Arguments:
- tokens: bfloat16 [65536, 2048], P(('dp', 'expert')), may hold values from -6 to 6
- out_grad: bfloat16 [65536, 2048], P(('dp', 'expert')), may hold values from -6 to 6
- expert_ids: int32 [65536, 6], P(('dp', 'expert')), may hold values from 0 to 63, all different within a row; in each aligned block of 128 rows (0 to 127, 128 to 255, ...) at most 14 rows name the same one
- route_weights: bfloat16 [65536, 6], P(('dp', 'expert')), may hold values from 0.019897461 to 0.5
- blocks: bfloat16 [64, 3, 12, 128, 128], P('expert'), may hold values from -0.5 to 0.5
- layout: int32 [64, 3, 12, 2], P('expert'), may hold values from 0 to 15, as said below
- moments: float32 [64, 3, 12, 128, 128], P('expert', None, None, 'dp'), may hold values from -12 to 12
- partner: int32 [64], replicated, may hold values from 0 to 63, as said below
Outputs:
- token_grad: bfloat16 [65536, 2048], P(('dp', 'expert'))
- route_grad: bfloat16 [65536, 6], P(('dp', 'expert'))
- new_blocks: bfloat16 [64, 3, 12, 128, 128], P('expert')
- new_moments: float32 [64, 3, 12, 128, 128], P('expert', None, None, 'dp')
The draws below stay inside these ranges and needn't reach their ends.
Inputs may be any that keep to these rules, and one draw needn't show every extreme that they name: `layout`: within one expert and matrix the stored blocks are at distinct places; for gate and up an entry is (block of the 2048 features, block of the 1408 hidden units), for down (block of the hidden units, block of the features). partner pairs the experts: partner[partner[e]] == e and partner[e] != e. `expert_ids`: each row names 6 different experts; among the rows of one device no expert is named more than 14 times, a bound that some block reaches.
All inputs are finite; a program needn't handle non-finite values.
Results may differ from the reference program's by a relative error of at most 0.0064.
Values may be sent and summed in bfloat16 or wider, within the bound.
A program may use at most 128 MiB of HBM per device.

```python
import math
import jax
import jax.numpy as jnp
import numpy as np
from jax import lax

D = 2048
HID = 1408
TOPK = 6
BLK = 128
NB = 12
TOK_DEV = 128
EXPERTS = 64
CAP = 14
TOKENS = 65536
N_DP = 8
N_EXPERT = 64


def draw_layout(key, part):
    feat_blocks = D // BLK
    hidden_blocks = HID // BLK
    cell_count = feat_blocks * hidden_blocks
    matrix_keys = jax.random.split(jax.random.fold_in(key, 11), EXPERTS * 3)
    chosen = jax.vmap(lambda one_key: jax.random.permutation(one_key, cell_count)[:NB])(matrix_keys)
    chosen = chosen.reshape(EXPERTS, 3, NB).astype(jnp.int32)
    first_rows = chosen[:, :2] // hidden_blocks
    first_cols = chosen[:, :2] % hidden_blocks
    down_rows = chosen[:, 2:] // feat_blocks
    down_cols = chosen[:, 2:] % feat_blocks
    row_part = jnp.concatenate([first_rows, down_rows], axis=1)
    col_part = jnp.concatenate([first_cols, down_cols], axis=1)
    return jnp.stack([row_part, col_part], axis=-1).astype(jnp.int32)


def draw_partner(key, part):
    order = jax.random.permutation(jax.random.fold_in(key, 23), EXPERTS).astype(jnp.int32)
    evens = order[0::2]
    odds = order[1::2]
    paired = jnp.zeros((EXPERTS,), jnp.int32).at[evens].set(odds).at[odds].set(evens)
    return paired


def block_levels(key, shape, cuts, smallest, top_value):
    gain, own = 1.0, jax.random.fold_in(key, 6)
    for dim, parts in cuts:
        heights = jnp.exp(jax.random.uniform(jax.random.fold_in(own, dim), (parts,), jnp.float32, smallest / len(cuts), top_value / len(cuts)))
        gain = gain * jnp.repeat(heights, shape[dim] // parts).reshape([-1 if axis == dim else 1 for axis in range(len(shape))])
    return gain


def shared_out(key, own, number, rows, amount, top, reach, skew):
    ranking = jax.random.permutation(key, amount)
    heavy_load, common = shares(amount, rows * top, reach, skew, True), shares(amount, rows * top, reach, skew, False)
    places = jnp.arange(amount)

    def named(sizes, offset_by):
        used = int((sizes > 0).sum())
        fixed = max(1, used // 4)
        moved = fixed + (places - fixed + offset_by * (used - fixed)) % max(1, amount - fixed)
        return jnp.zeros((amount,), jnp.int32).at[ranking[jnp.where(places < fixed, places, moved)]].set(jnp.asarray(sizes, jnp.int32))

    sizes = jnp.where(number % 4 == 0, named(heavy_load, number // 4), named(common, number - number // 4 - 1))
    mixed = jax.random.permutation(jax.random.fold_in(own, 3), amount)
    source_of, receiver = mixed[0:amount // 2 * 2:2], mixed[1:amount // 2 * 2:2]
    room = jnp.minimum(sizes[source_of] - 1, reach - sizes[receiver]) // 2
    room = jnp.where((source_of == ranking[0]) | (receiver == ranking[0]) | (sizes[receiver] == 0), 0, jnp.maximum(room, 0))
    moved = jax.random.randint(jax.random.fold_in(own, 4), (amount // 2,), 0, 1 << 20) % (room + 1)
    sizes = sizes.at[source_of].add(-moved).at[receiver].add(moved)
    items = jnp.searchsorted(jnp.cumsum(sizes), jnp.arange(rows * top), side="right").astype(jnp.int32)
    table = items.reshape(top, rows).T
    table = table[jax.random.permutation(jax.random.fold_in(own, 1), rows)]
    offset_by = jax.random.randint(jax.random.fold_in(own, 2), (rows, 1), 0, top)
    return jnp.take_along_axis(table, (jnp.arange(top)[None, :] + offset_by) % top, axis=1)


def shares(amount, total, bound, lean, full):
    weights = [(1 << 20) // math.isqrt(rank ** lean) + 1 for rank in range(1, amount + 1)]
    largest = bound if full else min(bound, max(-(-total // amount), total * weights[0] // sum(weights)))
    least = 1 if total - largest >= amount - 1 else 0
    holding, rest = [largest] + [least] * (amount - 1), total - largest - least * (amount - 1)
    while rest > 0:
        candidates = [i for i in range(1, amount) if holding[i] < largest] or [i for i in range(1, amount) if holding[i] < bound]
        whole, remaining = sum([weights[i] for i in candidates]), rest
        for i in candidates:
            more = min(bound - holding[i], max(1, remaining * weights[i] // whole), rest)
            holding[i] = holding[i] + more
            rest = rest - more
    return np.array(holding)


def centred(stream_key, shape, deviation, bound, cuts=(), kind=jnp.bfloat16):
    result = deviation * jax.random.normal(stream_key, shape, jnp.float32)
    if cuts:
        result = result * block_levels(stream_key, shape, cuts, -0.22, 0.18)
    return jnp.clip(result, -bound, bound).astype(kind)


def setup_inputs(seed: int = 0) -> dict:
    key_list = jax.random.split(jax.random.key(seed), 9)
    tokens = centred(key_list[0], (TOKENS, D), 1.0, 6.0, ((0, 512),))
    out_grad = centred(key_list[1], (TOKENS, D), 1.0, 6.0, ((0, 512),))
    expert_ids_keys = jax.random.split(jax.random.fold_in(key_list[2], 1), TOKENS // TOK_DEV)
    expert_ids_turns = jax.random.permutation(jax.random.fold_in(key_list[2], 3), TOKENS // TOK_DEV)
    expert_ids = jax.vmap(lambda own, number: shared_out(jax.random.fold_in(key_list[2], 2), own, number, TOK_DEV, EXPERTS, TOPK, CAP, 2))(expert_ids_keys, expert_ids_turns).reshape((TOKENS, TOPK))
    route_weights = jnp.clip(jnp.exp(math.log(0.5) - 3.224016 * jax.random.uniform(key_list[3], (TOKENS, TOPK), jnp.float32) ** block_levels(key_list[3], (TOKENS, TOPK), ((0, 512),), -0.2, 0.2)), 0.019897461, 0.5).astype(jnp.bfloat16)
    blocks = centred(key_list[4], (EXPERTS, 3, NB, BLK, BLK), BLK ** -0.5, 0.5, ((0, 64),))
    layout = draw_layout(jax.random.fold_in(key_list[8], 71), 0)
    moments = centred(key_list[6], (EXPERTS, 3, NB, BLK, BLK), 2.0, 12.0, ((0, 64), (3, 8)), jnp.float32)
    partner = draw_partner(jax.random.fold_in(key_list[8], 71), 0)
    return {"tokens": tokens, "out_grad": out_grad, "expert_ids": expert_ids, "route_weights": route_weights, "blocks": blocks, "layout": layout, "moments": moments, "partner": partner}


momentum_decay = 0.9
step_rate = 0.01


def block_product(left, mats, source_idx, target_idx, target_count, flipped):
    row_count = left.shape[0]
    block_size = mats.shape[-1]
    pieces = jnp.take(left.reshape(row_count, -1, block_size), source_idx, axis=1).astype(jnp.float32)
    wide = mats.astype(jnp.float32)
    if flipped:
        partial_out = jnp.einsum("rbk,bnk->rbn", pieces, wide, precision=lax.Precision.HIGHEST)
    else:
        partial_out = jnp.einsum("rbk,bkn->rbn", pieces, wide, precision=lax.Precision.HIGHEST)
    select = (target_idx[:, None] == jnp.arange(target_count, dtype=jnp.int32)[None, :]).astype(jnp.float32)
    placed = jnp.einsum("rbn,bc->rcn", partial_out, select, precision=lax.Precision.HIGHEST)
    return placed.reshape(row_count, target_count * block_size)


def block_outer(left, right, left_idx, right_idx, block_size):
    row_count = left.shape[0]
    left_pieces = jnp.take(left.reshape(row_count, -1, block_size), left_idx, axis=1).astype(jnp.float32)
    right_pieces = jnp.take(right.reshape(row_count, -1, block_size), right_idx, axis=1).astype(jnp.float32)
    return jnp.einsum("rbk,rbn->bkn", left_pieces, right_pieces, precision=lax.Precision.HIGHEST)


def expert_forward(inputs, matrices, layout_one, hidden_blocks, feat_blocks):
    gate_pre = block_product(inputs, matrices[0], layout_one[0, :, 0], layout_one[0, :, 1], hidden_blocks, False)
    up_pre = block_product(inputs, matrices[1], layout_one[1, :, 0], layout_one[1, :, 1], hidden_blocks, False)
    sigmoid_gate = jax.nn.sigmoid(gate_pre)
    activated = gate_pre * sigmoid_gate
    hidden = (activated * up_pre).astype(jnp.bfloat16)
    output = block_product(hidden, matrices[2], layout_one[2, :, 0], layout_one[2, :, 1], feat_blocks, False)
    return (gate_pre, up_pre, sigmoid_gate, activated, hidden, output)


def expert_backward(inputs, upstream, weights_col, matrices, layout_one, hidden_blocks, feat_blocks, saved):
    gate_pre, up_pre, sigmoid_gate, activated, hidden, output = saved
    score = jnp.sum(output * upstream.astype(jnp.float32), axis=1).astype(jnp.bfloat16)
    scaled = (weights_col.astype(jnp.float32)[:, None] * upstream.astype(jnp.float32)).astype(jnp.bfloat16)
    hidden_grad = block_product(scaled, matrices[2], layout_one[2, :, 1], layout_one[2, :, 0], hidden_blocks, True)
    gate_grad = (hidden_grad * up_pre * sigmoid_gate * (1.0 + gate_pre * (1.0 - sigmoid_gate))).astype(jnp.bfloat16)
    up_grad = (hidden_grad * activated).astype(jnp.bfloat16)
    input_grad = (block_product(gate_grad, matrices[0], layout_one[0, :, 1], layout_one[0, :, 0], feat_blocks, True)
                  + block_product(up_grad, matrices[1], layout_one[1, :, 1], layout_one[1, :, 0], feat_blocks, True)).astype(jnp.bfloat16)
    block_size = matrices.shape[-1]
    weight_grad = jnp.stack([
        block_outer(inputs, gate_grad, layout_one[0, :, 0], layout_one[0, :, 1], block_size),
        block_outer(inputs, up_grad, layout_one[1, :, 0], layout_one[1, :, 1], block_size),
        block_outer(hidden, scaled, layout_one[2, :, 0], layout_one[2, :, 1], block_size)])
    return score, input_grad, weight_grad


def reference(tokens, out_grad, expert_ids, route_weights, blocks, layout, moments, partner):
    pick_total = TOKENS * TOPK
    flat_ids = expert_ids.reshape(-1)
    order = jnp.argsort(flat_ids, stable=True).astype(jnp.int32)
    counts = jnp.bincount(flat_ids, length=EXPERTS).astype(jnp.int32)
    starts = (jnp.cumsum(counts) - counts).astype(jnp.int32)
    most_rows = CAP * N_DP * N_EXPERT
    padded_order = jnp.concatenate([order, jnp.full((most_rows,), pick_total, jnp.int32)])
    feat_blocks = D // BLK
    hidden_blocks = HID // BLK
    flat_weights = route_weights.reshape(-1)

    def per_expert(carry, expert):
        grad_total, score_total = carry
        position = lax.dynamic_slice_in_dim(padded_order, starts[expert].astype(jnp.int32), most_rows)
        filled = jnp.arange(most_rows, dtype=jnp.int32) < counts[expert]
        safe_pick = jnp.minimum(position, pick_total - 1).astype(jnp.int32)
        token_of = (safe_pick // TOPK).astype(jnp.int32)
        inputs = jnp.where(filled[:, None], tokens[token_of], jnp.zeros((), tokens.dtype))
        upstream = jnp.where(filled[:, None], out_grad[token_of], jnp.zeros((), out_grad.dtype))
        weights_col = jnp.where(filled, flat_weights[safe_pick], jnp.zeros((), route_weights.dtype))
        matrices = blocks[expert]
        layout_one = layout[expert]
        saved = expert_forward(inputs, matrices, layout_one, hidden_blocks, feat_blocks)
        score, input_grad, weight_grad = expert_backward(inputs, upstream, weights_col, matrices, layout_one, hidden_blocks, feat_blocks, saved)
        target = jnp.where(filled, token_of, TOKENS).astype(jnp.int32)
        grad_total = grad_total.at[target].add(input_grad.astype(jnp.float32), mode="drop")
        pick_target = jnp.where(filled, safe_pick, pick_total).astype(jnp.int32)
        score_total = score_total.at[pick_target].set(score.astype(jnp.float32), mode="drop")
        return (grad_total, score_total), weight_grad

    start_carry = (jnp.zeros((TOKENS, D), jnp.float32), jnp.zeros((pick_total,), jnp.float32))
    (grad_total, score_total), weight_grads = lax.scan(per_expert, start_carry, jnp.arange(EXPERTS, dtype=jnp.int32))
    token_grad = grad_total.astype(jnp.bfloat16)
    route_grad = score_total.reshape(TOKENS, TOPK).astype(jnp.bfloat16)
    moment = momentum_decay * moments + weight_grads
    updated = (blocks.astype(jnp.float32) - step_rate * moment).astype(jnp.bfloat16)
    return token_grad, route_grad, updated[partner], moment[partner]
```

```python
import functools

import jax
import jax.numpy as jnp
from jax import lax
from jax.experimental import pallas as pl
from jax.experimental.pallas import tpu as pltpu
from jax.sharding import PartitionSpec as P

HID = 1408
BLK = 128
CAP = 14
DECAY = 0.9
RATE = 0.01

NT = (((1,), (1,)), ((), ()))
TN = (((0,), (0,)), ((), ()))


def dot(a, b, dims=(((1,), (0,)), ((), ()))):
    return lax.dot_general(a, b, dims, preferred_element_type=jnp.float32)


def lanes(i):
    return pl.ds(pl.multiple_of(i * BLK, BLK), BLK)


def expert_kernel(lay, x_ref, s_ref, w_ref, pg_ref, sc_ref, wg_ref, gate, up, hg, hid, gg, ug, acc):
    nb = w_ref.shape[1]
    rows = x_ref.shape[1]
    per = x_ref.shape[2] // BLK

    def chunk(ref, i):
        return ref[i // per, :, lanes(i % per)]

    @pl.when(pl.program_id(0) == 0)
    def _():
        wg_ref[...] = jnp.zeros_like(wg_ref)

    gate[...] = jnp.zeros_like(gate)
    up[...] = jnp.zeros_like(up)
    hg[...] = jnp.zeros_like(hg)

    def first(b, carry):
        gate[:, lanes(lay[0, b, 1])] += dot(chunk(x_ref, lay[0, b, 0]), w_ref[0, b])
        up[:, lanes(lay[1, b, 1])] += dot(chunk(x_ref, lay[1, b, 0]), w_ref[1, b])
        hg[:, lanes(lay[2, b, 0])] += dot(chunk(s_ref, lay[2, b, 1]), w_ref[2, b], NT)
        return carry

    lax.fori_loop(0, nb, first, 0)

    def middle(j, score):
        g = gate[:, lanes(j)]
        u = up[:, lanes(j)]
        h = hg[:, lanes(j)]
        sig = jax.nn.sigmoid(g)
        act = g * sig
        hb = (act * u).astype(jnp.bfloat16)
        hid[:, lanes(j)] = hb
        gg[:, lanes(j)] = (h * u * sig * (1.0 + g * (1.0 - sig))).astype(jnp.bfloat16)
        ug[:, lanes(j)] = (h * act).astype(jnp.bfloat16)
        return score + hb.astype(jnp.float32) * h

    score = lax.fori_loop(0, HID // BLK, middle, jnp.zeros((rows, BLK), jnp.float32))
    total = jnp.sum(score, axis=1, keepdims=True)
    high = total.astype(jnp.bfloat16).astype(jnp.float32)
    lane = lax.broadcasted_iota(jnp.int32, (rows, BLK), 1)
    place = 0
    sc_ref[...] = jnp.where(
        lane == place, high, jnp.where(lane == place + 8, total - high, 0.0)
    ).astype(jnp.bfloat16)

    acc[...] = jnp.zeros_like(acc)

    def last(b, carry):
        r0, c0, r1, c1 = lay[0, b, 0], lay[0, b, 1], lay[1, b, 0], lay[1, b, 1]
        acc[:, lanes(r0)] += dot(gg[:, lanes(c0)], w_ref[0, b], NT)
        acc[:, lanes(r1)] += dot(ug[:, lanes(c1)], w_ref[1, b], NT)
        wg_ref[0, b] += dot(chunk(x_ref, r0), gg[:, lanes(c0)], TN)
        wg_ref[1, b] += dot(chunk(x_ref, r1), ug[:, lanes(c1)], TN)
        wg_ref[2, b] += dot(hid[:, lanes(lay[2, b, 0])], chunk(s_ref, lay[2, b, 1]), TN)
        return carry

    lax.fori_loop(0, nb, last, 0)
    for q in range(pg_ref.shape[0]):
        width = pg_ref.shape[2]
        pg_ref[q] = acc[:, q * width : (q + 1) * width].astype(jnp.bfloat16)


def expert_compute(layout_one, xs, grads, mats, tile):
    nq, rows, width = xs.shape
    nm, nb = mats.shape[:2]
    row_spec = pl.BlockSpec((nq, tile, width), lambda i, lay: (0, i, 0))
    f32, bf16 = jnp.float32, jnp.bfloat16
    return pl.pallas_call(
        expert_kernel,
        grid_spec=pltpu.PrefetchScalarGridSpec(
            num_scalar_prefetch=1,
            grid=(rows // tile,),
            in_specs=[
                row_spec,
                row_spec,
                pl.BlockSpec((nm, nb, BLK, BLK), lambda i, lay: (0, 0, 0, 0)),
            ],
            out_specs=[
                row_spec,
                pl.BlockSpec((tile, BLK), lambda i, lay: (i, 0)),
                pl.BlockSpec((nm, nb, BLK, BLK), lambda i, lay: (0, 0, 0, 0)),
            ],
            scratch_shapes=[
                pltpu.VMEM((tile, HID), f32),
                pltpu.VMEM((tile, HID), f32),
                pltpu.VMEM((tile, HID), f32),
                pltpu.VMEM((tile, HID), bf16),
                pltpu.VMEM((tile, HID), bf16),
                pltpu.VMEM((tile, HID), bf16),
                pltpu.VMEM((tile, nq * width), f32),
            ],
        ),
        out_shape=[
            jax.ShapeDtypeStruct(xs.shape, bf16),
            jax.ShapeDtypeStruct((rows, BLK), bf16),
            jax.ShapeDtypeStruct(mats.shape, f32),
        ],
        compiler_params=pltpu.CompilerParams(vmem_limit_bytes=56 << 20),
        cost_estimate=pl.CostEstimate(
            flops=8 * nb * rows * BLK * BLK * 2,
            bytes_accessed=3 * xs.size * 2 + mats.size * 6,
            transcendentals=rows * HID,
        ),
    )(layout_one, xs, grads, mats)


def move_state(own_blocks, moments, layout_one, partner, n):
    bf16 = jnp.bfloat16
    tiles = own_blocks.size // (16 * BLK)
    high = moments.astype(bf16)
    low = (moments - high.astype(jnp.float32)).astype(bf16)
    flat_layout = layout_one.reshape(-1)
    lay_tile = jnp.pad(flat_layout, (0, 16 * BLK - flat_layout.size)).astype(bf16)
    count = 3 * tiles + 1
    padded = -(-count // n) * n
    state = jnp.concatenate(
        [
            own_blocks.reshape(tiles, 16, BLK),
            high.reshape(tiles, 16, BLK),
            low.reshape(tiles, 16, BLK),
            lay_tile.reshape(1, 16, BLK),
            jnp.zeros((padded - count, 16, BLK), bf16),
        ]
    ).reshape(n, -1, BLK)
    spread = lax.all_to_all(state, "expert", split_axis=0, concat_axis=0, tiled=True)
    moved = lax.all_to_all(spread[partner], "expert", split_axis=0, concat_axis=0, tiled=True)
    moved = moved.reshape(padded, 16, BLK)
    new_blocks = moved[:tiles].reshape(own_blocks.shape)
    new_moments = (
        moved[tiles : 2 * tiles].astype(jnp.float32)
        + moved[2 * tiles : 3 * tiles].astype(jnp.float32)
    ).reshape(moments.shape)
    new_layout = (
        moved[3 * tiles].reshape(-1)[: flat_layout.size].astype(jnp.int32).reshape(layout_one.shape)
    )
    return new_blocks, new_moments, new_layout


def body(tokens, out_grad, expert_ids, route_weights, blocks, layout, moments, partner):
    f32, bf16 = jnp.float32, jnp.bfloat16
    n = lax.axis_size("expert")
    n_dp = lax.axis_size("dp")
    count, width = tokens.shape
    share = BLK // n_dp
    own = lax.dynamic_slice_in_dim(blocks[0], lax.axis_index("dp") * share, share, 2)
    own, old_moment, layout_one = move_state(own, moments[0], layout[0], partner, n)
    mats = lax.all_gather(own, "dp", axis=2, tiled=True)

    picks = expert_ids[None] == partner[:, None, None]
    named = jnp.any(picks, axis=2)
    before = jnp.tril(jnp.ones((count, count), bf16), -1)
    rank = dot(named.astype(bf16), before, NT)
    rank = jnp.where(named, rank, -1.0)
    weight = jnp.sum(jnp.where(picks, route_weights[None].astype(f32), 0.0), axis=2)
    slots = lax.broadcasted_iota(jnp.int32, (1, CAP, 1), 1).astype(f32)
    choose = rank[:, None, :] == slots
    take = choose.astype(bf16).reshape(n * CAP, count)
    scale = jnp.where(choose, weight[:, None, :], 0.0).astype(bf16).reshape(n * CAP, count)
    send_x = dot(take, tokens).astype(bf16).reshape(n, CAP, width)
    send_s = dot(scale, out_grad).astype(bf16).reshape(n, CAP, width)
    xs = lax.all_to_all(send_x, "expert", split_axis=0, concat_axis=0, tiled=True)
    ss = lax.all_to_all(send_s, "expert", split_axis=0, concat_axis=0, tiled=True)
    pg, sc, wg = expert_compute(
        layout_one, xs.reshape(1, n * CAP, width), ss.reshape(1, n * CAP, width), mats, 448
    )
    back = jnp.concatenate([pg[0], sc], axis=1).reshape(n, CAP, width + BLK)
    back = lax.all_to_all(back, "expert", split_axis=0, concat_axis=0, tiled=True)
    back = back.reshape(n * CAP, width + BLK)
    token_grad = dot(take, back[:, :width], TN).astype(bf16)
    score_rows = back[:, width].astype(f32) + back[:, width + 8].astype(f32)
    score = jnp.sum(jnp.where(choose, score_rows.reshape(n, CAP, 1), 0.0), axis=1)
    score = jnp.sum(jnp.where(picks, score[:, :, None], 0.0), axis=0)
    route_grad = (score / route_weights.astype(f32)).astype(bf16)

    shard = lax.psum_scatter(wg, "dp", scatter_dimension=2, tiled=True)
    moment = DECAY * old_moment + shard
    updated = (own.astype(f32) - RATE * moment).astype(bf16)
    gathered = lax.all_gather(updated, "dp", axis=2, tiled=True)
    return token_grad, route_grad, gathered[None], moment[None]


def solution(mesh):
    rows = P(("dp", "expert"), None)
    state = P("expert", None, None, None, None)
    moment = P("expert", None, None, "dp", None)
    return jax.shard_map(
        body,
        mesh=mesh,
        in_specs=(rows, rows, rows, rows, state, P("expert", None, None, None), moment, P()),
        out_specs=(rows, rows, state, moment),
        check_vma=False,
    )
```

```python
import functools

import jax
import jax.numpy as jnp
from jax import lax
from jax.experimental import pallas as pl
from jax.experimental.pallas import tpu as pltpu
from jax.sharding import PartitionSpec as P

HID = 1408
BLK = 128
CAP = 14
DECAY = 0.9
RATE = 0.01

NT = (((1,), (1,)), ((), ()))
TN = (((0,), (0,)), ((), ()))


def dot(a, b, dims=(((1,), (0,)), ((), ()))):
    return lax.dot_general(a, b, dims, preferred_element_type=jnp.float32)


def lanes(i):
    return pl.ds(pl.multiple_of(i * BLK, BLK), BLK)


def expert_kernel(lay, place_ref, x_ref, s_ref, w_ref, pg_ref, sc_ref, wg_ref, gate, up, hg, hid, gg, ug, acc):
    nb = w_ref.shape[1]
    rows = x_ref.shape[1]
    per = x_ref.shape[2] // BLK

    def chunk(ref, i):
        return ref[i // per, :, lanes(i % per)]

    @pl.when(pl.program_id(0) == 0)
    def _():
        wg_ref[...] = jnp.zeros_like(wg_ref)

    gate[...] = jnp.zeros_like(gate)
    up[...] = jnp.zeros_like(up)
    hg[...] = jnp.zeros_like(hg)

    def first(b, carry):
        gate[:, lanes(lay[0, b, 1])] += dot(chunk(x_ref, lay[0, b, 0]), w_ref[0, b])
        up[:, lanes(lay[1, b, 1])] += dot(chunk(x_ref, lay[1, b, 0]), w_ref[1, b])
        hg[:, lanes(lay[2, b, 0])] += dot(chunk(s_ref, lay[2, b, 1]), w_ref[2, b], NT)
        return carry

    lax.fori_loop(0, nb, first, 0)

    def middle(j, score):
        g = gate[:, lanes(j)]
        u = up[:, lanes(j)]
        h = hg[:, lanes(j)]
        sig = jax.nn.sigmoid(g)
        act = g * sig
        hb = (act * u).astype(jnp.bfloat16)
        hid[:, lanes(j)] = hb
        gg[:, lanes(j)] = (h * u * sig * (1.0 + g * (1.0 - sig))).astype(jnp.bfloat16)
        ug[:, lanes(j)] = (h * act).astype(jnp.bfloat16)
        return score + hb.astype(jnp.float32) * h

    score = lax.fori_loop(0, HID // BLK, middle, jnp.zeros((rows, BLK), jnp.float32))
    total = jnp.sum(score, axis=1, keepdims=True)
    high = total.astype(jnp.bfloat16).astype(jnp.float32)
    lane = lax.broadcasted_iota(jnp.int32, (rows, BLK), 1)
    place = place_ref[0]
    sc_ref[...] = jnp.where(
        lane == place, high, jnp.where(lane == place + 8, total - high, 0.0)
    ).astype(jnp.bfloat16)

    acc[...] = jnp.zeros_like(acc)

    def last(b, carry):
        r0, c0, r1, c1 = lay[0, b, 0], lay[0, b, 1], lay[1, b, 0], lay[1, b, 1]
        acc[:, lanes(r0)] += dot(gg[:, lanes(c0)], w_ref[0, b], NT)
        acc[:, lanes(r1)] += dot(ug[:, lanes(c1)], w_ref[1, b], NT)
        wg_ref[0, b] += dot(chunk(x_ref, r0), gg[:, lanes(c0)], TN)
        wg_ref[1, b] += dot(chunk(x_ref, r1), ug[:, lanes(c1)], TN)
        wg_ref[2, b] += dot(hid[:, lanes(lay[2, b, 0])], chunk(s_ref, lay[2, b, 1]), TN)
        return carry

    lax.fori_loop(0, nb, last, 0)
    for q in range(pg_ref.shape[0]):
        width = pg_ref.shape[2]
        pg_ref[q] = acc[:, q * width : (q + 1) * width].astype(jnp.bfloat16)


def expert_compute(layout_one, place, xs, mats, tile):
    nq, rows, width = xs.shape
    nq = nq // 2
    nm, nb = mats.shape[:2]
    row_spec = pl.BlockSpec((nq, tile, width), lambda i, lay, place: (0, i, 0))
    grad_spec = pl.BlockSpec((nq, tile, width), lambda i, lay, place: (1, i, 0))
    f32, bf16 = jnp.float32, jnp.bfloat16
    return pl.pallas_call(
        expert_kernel,
        grid_spec=pltpu.PrefetchScalarGridSpec(
            num_scalar_prefetch=2,
            grid=(rows // tile,),
            in_specs=[
                row_spec,
                grad_spec,
                pl.BlockSpec((nm, nb, BLK, BLK), lambda i, lay, place: (0, 0, 0, 0)),
            ],
            out_specs=[
                row_spec,
                pl.BlockSpec((tile, BLK), lambda i, lay, place: (i, 0)),
                pl.BlockSpec((nm, nb, BLK, BLK), lambda i, lay, place: (0, 0, 0, 0)),
            ],
            scratch_shapes=[
                pltpu.VMEM((tile, HID), f32),
                pltpu.VMEM((tile, HID), f32),
                pltpu.VMEM((tile, HID), f32),
                pltpu.VMEM((tile, HID), bf16),
                pltpu.VMEM((tile, HID), bf16),
                pltpu.VMEM((tile, HID), bf16),
                pltpu.VMEM((tile, nq * width), f32),
            ],
        ),
        out_shape=[
            jax.ShapeDtypeStruct((nq, rows, width), bf16),
            jax.ShapeDtypeStruct((rows, BLK), bf16),
            jax.ShapeDtypeStruct(mats.shape, f32),
        ],
        compiler_params=pltpu.CompilerParams(vmem_limit_bytes=56 << 20),
        cost_estimate=pl.CostEstimate(
            flops=8 * nb * rows * BLK * BLK * 2,
            bytes_accessed=3 * xs.size + mats.size * 6,
            transcendentals=rows * HID,
        ),
    )(layout_one, place, xs, xs, mats)


NX, NZ, NCORE = 4, 8, 2
PLANE = NX * NCORE
ROWS = NZ * CAP
MESH = pl.DeviceIdType.MESH


def position():
    me = lax.axis_index("expert")
    return lax.axis_index("dp"), me // (NZ * NCORE), (me // NCORE) % NZ, me % NCORE


def peers():
    dp, x, z, core = position()

    def along(other):
        return (dp, x * (NZ * NCORE) + other * NCORE + core)

    def across(other):
        return (dp, (other // NCORE) * (NZ * NCORE) + z * NCORE + other % NCORE)

    return z, x * NCORE + core, along, across


def meet(z, j, along, across):
    barrier = pltpu.get_barrier_semaphore()
    for k in range(1, NZ):
        pl.semaphore_signal(barrier, inc=1, device_id=along((z + k) % NZ), device_id_type=MESH)
    for k in range(1, PLANE):
        pl.semaphore_signal(barrier, inc=1, device_id=across((j + k) % PLANE), device_id_type=MESH)
    pl.semaphore_wait(barrier, NZ + PLANE - 2)


def send(src, dst, send_sem, recv_sem, device):
    return pltpu.make_async_remote_copy(
        src_ref=src,
        dst_ref=dst,
        send_sem=send_sem,
        recv_sem=recv_sem,
        device_id=device,
        device_id_type=MESH,
    )


def span(i, size):
    return pl.ds(pl.multiple_of(i * size, size), size)


def dispatch_kernel(
    tok, og, meta, xs, chosen, ring, picked, choose, notes,
    own_sem, notes_send, notes_recv, ring_send, ring_recv, out_send, out_recv, out_own, keep_sem,
):
    count = tok.shape[0]
    chunks, _, width = ring.shape
    half = chunks // 2
    z, j, along, across = peers()
    ahead, behind = along((z + 1) % NZ), along((z + NZ - 1) % NZ)

    def own_copy(q):
        src = tok if q < half else og
        return pltpu.make_async_copy(
            src.at[:, (q % half) * width : (q % half + 1) * width],
            ring.at[q, span(z, count)],
            own_sem.at[q],
        )

    for q in range(chunks):
        own_copy(q).start()
    own_notes = pltpu.make_async_copy(meta.at[z], notes.at[z], keep_sem.at[1])
    own_notes.start()
    meet(z, j, along, across)

    def note(k, source):
        return send(
            meta.at[(z + k) % NZ],
            notes.at[source],
            notes_send.at[k],
            notes_recv.at[k],
            along((z + k) % NZ),
        )

    for k in range(1, NZ):
        note(k, z).start()
    for q in range(chunks):
        own_copy(q).wait()
    own_notes.wait()

    def hop(q, way, step, arriving):
        rows = count
        if way == 0:
            source = (z + 2 * NZ - step - (1 if arriving else 0)) % NZ
        else:
            source = (z + step + (1 if arriving else 0)) % NZ
        start = source * count
        if step == NZ // 2 - 1:
            rows = count // 2
            start = start + way * rows
        block = ring.at[q, pl.ds(pl.multiple_of(start, rows), rows)]
        return send(
            block, block, ring_send.at[q, way, step], ring_recv.at[q, way, step], ahead if way == 0 else behind
        )

    def out(q, other, landing):
        step = (other + PLANE - j) % PLANE
        return send(
            picked.at[q, span(other, ROWS)],
            xs.at[q, span(landing, ROWS)],
            out_send.at[q, step],
            out_recv.at[q, step],
            across(other),
        )

    def own_out(q):
        return pltpu.make_async_copy(
            picked.at[q, span(j, ROWS)], xs.at[q, span(j, ROWS)], out_own.at[q]
        )

    def keep():
        return pltpu.make_async_copy(choose.at[0], chosen, keep_sem.at[0])

    def build():
        for k in range(1, NZ):
            note(k, (z + NZ - k) % NZ).wait_recv()
        row = lax.broadcasted_iota(jnp.int32, (ROWS, count), 0).astype(jnp.float32)

        def fill(source, carry):
            both = notes[source].astype(jnp.float32)
            for other in range(PLANE):
                hit = row == both[other : other + 1, :]
                rows = slice(other * ROWS, (other + 1) * ROWS)
                scale = both[PLANE + other : PLANE + other + 1, :]
                choose[0, rows, span(source, count)] = jnp.where(hit, 1.0, 0.0).astype(jnp.bfloat16)
                choose[1, rows, span(source, count)] = jnp.where(hit, scale, 0.0).astype(jnp.bfloat16)
            return carry

        lax.fori_loop(0, NZ, fill, 0)
        keep().start()

    def step(i, carry):
        for s in range(NZ // 2):
            q = i - s

            @pl.when((q >= 0) & (q < chunks))
            def _():
                for way in range(2):
                    if s:
                        hop(q, way, s - 1, True).wait_recv()
                    hop(q, way, s, False).start()

        pl.when(i == 1)(build)
        q = i - NZ // 2

        @pl.when(q >= 0)
        def _():
            for way in range(2):
                hop(q, way, NZ // 2 - 1, True).wait_recv()

            def part(h, carry):
                rows = span(h, PLANE // 2 * ROWS)
                picked[q, rows, :] = dot(choose[q // half, rows, :], ring[q]).astype(jnp.bfloat16)
                for o in range(PLANE // 2):
                    other = h * (PLANE // 2) + o

                    @pl.when(other != j)
                    def _():
                        out(q, other, j).start()

                return carry

            lax.fori_loop(0, 2, part, 0)
            own_out(q).start()

        return carry

    lax.fori_loop(0, chunks + NZ // 2, step, 0)

    def finish(q, carry):
        for way in range(2):
            for s in range(NZ // 2):
                hop(q, way, s, False).wait_send()
        for o in range(1, PLANE):
            out(q, (j + o) % PLANE, j).wait_send()
            out(q, (j + o) % PLANE, (j + PLANE - o) % PLANE).wait_recv()
        own_out(q).wait()
        return carry

    lax.fori_loop(0, chunks, finish, 0)
    for k in range(1, NZ):
        note(k, z).wait_send()
    keep().wait()


def dispatch(tokens, grads, meta, chunks):
    count, features = tokens.shape
    width = 2 * features // chunks
    bf16 = jnp.bfloat16
    slots = PLANE * ROWS
    dma = pltpu.SemaphoreType.DMA
    anywhere = pl.BlockSpec(memory_space=pl.ANY)
    return pl.pallas_call(
        dispatch_kernel,
        in_specs=[anywhere, anywhere, anywhere],
        out_specs=[anywhere, anywhere],
        out_shape=[
            jax.ShapeDtypeStruct((chunks, slots, width), bf16),
            jax.ShapeDtypeStruct((slots, NZ * count), bf16),
        ],
        scratch_shapes=[
            pltpu.VMEM((chunks, NZ * count, width), bf16),
            pltpu.VMEM((chunks, slots, width), bf16),
            pltpu.VMEM((2, slots, NZ * count), bf16),
            pltpu.VMEM(meta.shape, bf16),
            dma((chunks,)),
            dma((NZ,)),
            dma((NZ,)),
            dma((chunks, 2, NZ // 2)),
            dma((chunks, 2, NZ // 2)),
            dma((chunks, PLANE)),
            dma((chunks, PLANE)),
            dma((chunks,)),
            dma((2,)),
        ],
        compiler_params=pltpu.CompilerParams(
            collective_id=0, has_side_effects=True, vmem_limit_bytes=56 << 20
        ),
        cost_estimate=pl.CostEstimate(flops=2 * slots * NZ * count * 2 * features, bytes_accessed=300 << 20, transcendentals=0),
    )(tokens, grads, meta)


def return_kernel(
    pg, sc, choose, tg, score, back, marks, part, leaving, landed, sums,
    own_sem, x_send, x_recv, mark_send, mark_recv, z_send, z_recv, sum_send, sum_recv,
):
    chunks, slots, width = pg.shape
    count = tg.shape[0]
    last = NZ // 2 - 1
    z, j, along, across = peers()
    ahead, behind = along((z + 1) % NZ), along((z + NZ - 1) % NZ)

    def own_copy(q):
        return pltpu.make_async_copy(
            pg.at[q, span(j, ROWS)], back.at[q, span(j, ROWS)], own_sem.at[q]
        )

    own_marks = pltpu.make_async_copy(sc.at[span(j, ROWS)], marks.at[span(j, ROWS)], own_sem.at[chunks])
    for q in range(chunks):
        own_copy(q).start()
    own_marks.start()
    meet(z, j, along, across)

    def cross(q, o, landing):
        other = (j + o) % PLANE
        return send(
            pg.at[q, span(other, ROWS)],
            back.at[q, span(landing, ROWS)],
            x_send.at[q, o],
            x_recv.at[q, o],
            across(other),
        )

    def mark(o, landing):
        other = (j + o) % PLANE
        return send(
            sc.at[span(other, ROWS)],
            marks.at[span(landing, ROWS)],
            mark_send.at[o],
            mark_recv.at[o],
            across(other),
        )

    def start_cross(q, carry):
        for o in range(1, PLANE):
            cross(q, o, j).start()
        return carry

    lax.fori_loop(0, chunks, start_cross, 0)
    for o in range(1, PLANE):
        mark(o, j).start()
    for q in range(chunks):
        own_copy(q).wait()
    own_marks.wait()

    def hop(q, way, step):
        rows = slice(0, count)
        if step == 0:
            rows = slice(way * (count // 2), (way + 1) * (count // 2))
        return send(
            leaving.at[q, way, step, rows],
            landed.at[q, way, step, rows],
            z_send.at[q, way, step],
            z_recv.at[q, way, step],
            ahead if way == 0 else behind,
        )

    def target(way, step):
        if way == 0:
            return (z + NZ // 2 - step) % NZ
        return (z + NZ // 2 + step) % NZ

    def step(i, carry):
        @pl.when(i < chunks)
        def _():
            q = i
            for o in range(1, PLANE):
                cross(q, o, (j + PLANE - o) % PLANE).wait_recv()

            def add(t, carry):
                cols = span(t, 2 * count)
                part[q, cols, :] = dot(choose[:, cols], back[q], TN)
                return carry

            lax.fori_loop(0, NZ // 2, add, 0)
            for way in range(2):
                size = count // 2
                start = target(way, 0) * count + way * size
                rows = pl.ds(pl.multiple_of(start, size), size)
                leaving[q, way, 0, way * size : (way + 1) * size, :] = part[q, rows, :].astype(jnp.bfloat16)
                hop(q, way, 0).start()

        for s in range(1, NZ // 2):
            q = i - s

            @pl.when((q >= 0) & (q < chunks))
            def _():
                for way in range(2):
                    hop(q, way, s - 1).wait_recv()
                    mine = part[q, span(target(way, s), count), :]
                    if s == 1:
                        size = count // 2
                        near = slice(way * size, (way + 1) * size)
                        far = slice((1 - way) * size, (2 - way) * size)
                        more = landed[q, way, 0, near, :].astype(jnp.float32)
                        leaving[q, way, 1, near, :] = (mine[near] + more).astype(jnp.bfloat16)
                        leaving[q, way, 1, far, :] = mine[far].astype(jnp.bfloat16)
                    else:
                        more = landed[q, way, s - 1].astype(jnp.float32)
                        leaving[q, way, s] = (mine + more).astype(jnp.bfloat16)
                    hop(q, way, s).start()

        q = i - NZ // 2

        @pl.when(q >= 0)
        def _():
            total = part[q, span(z, count), :]
            for way in range(2):
                hop(q, way, last).wait_recv()
                total = total + landed[q, way, last].astype(jnp.float32)
            tg[:, pl.ds(pl.multiple_of(q * width, width), width)] = total.astype(jnp.bfloat16)

        @pl.when(i == chunks - 1)
        def _():
            for o in range(1, PLANE):
                mark(o, (j + PLANE - o) % PLANE).wait_recv()
            spread = dot(marks[...], choose[...], TN)
            both = spread[:PLANE] + spread[PLANE : 2 * PLANE]
            for source in range(NZ):
                sums[source] = both[:, source * count : (source + 1) * count]
            own_sum().start()
            for k in range(1, NZ):
                summed(k, z).start()

        return carry

    def own_sum():
        return pltpu.make_async_copy(sums.at[z], score.at[z], sum_send.at[0])

    def summed(k, landing):
        other = (z + k) % NZ
        return send(sums.at[other], score.at[landing], sum_send.at[k], sum_recv.at[k], along(other))

    lax.fori_loop(0, chunks + NZ // 2, step, 0)

    def finish(q, carry):
        for o in range(1, PLANE):
            cross(q, o, j).wait_send()
        for way in range(2):
            for s in range(NZ // 2):
                hop(q, way, s).wait_send()
        return carry

    lax.fori_loop(0, chunks, finish, 0)
    own_sum().wait()
    for o in range(1, PLANE):
        mark(o, j).wait_send()
    for k in range(1, NZ):
        summed(k, z).wait_send()
        summed(k, (z + NZ - k) % NZ).wait_recv()


def give_back(pg, sc, choose, count):
    chunks, slots, width = pg.shape
    f32, bf16 = jnp.float32, jnp.bfloat16
    dma = pltpu.SemaphoreType.DMA
    anywhere = pl.BlockSpec(memory_space=pl.ANY)
    vmem = pl.BlockSpec(memory_space=pltpu.VMEM)
    return pl.pallas_call(
        return_kernel,
        in_specs=[anywhere, anywhere, vmem],
        out_specs=[vmem, anywhere],
        out_shape=[
            jax.ShapeDtypeStruct((count, chunks * width), bf16),
            jax.ShapeDtypeStruct((NZ, PLANE, count), f32),
        ],
        scratch_shapes=[
            pltpu.VMEM((chunks, slots, width), bf16),
            pltpu.VMEM(sc.shape, bf16),
            pltpu.VMEM((chunks, NZ * count, width), f32),
            pltpu.VMEM((chunks, 2, NZ // 2, count, width), bf16),
            pltpu.VMEM((chunks, 2, NZ // 2, count, width), bf16),
            pltpu.VMEM((NZ, PLANE, count), f32),
            dma((chunks + 1,)),
            dma((chunks, PLANE)),
            dma((chunks, PLANE)),
            dma((PLANE,)),
            dma((PLANE,)),
            dma((chunks, 2, NZ // 2)),
            dma((chunks, 2, NZ // 2)),
            dma((NZ,)),
            dma((NZ,)),
        ],
        compiler_params=pltpu.CompilerParams(
            collective_id=1, has_side_effects=True, vmem_limit_bytes=56 << 20
        ),
        cost_estimate=pl.CostEstimate(flops=2 * slots * NZ * count * chunks * width, bytes_accessed=150 << 20, transcendentals=0),
    )(pg, sc, choose)


def move_state(own_blocks, moments, layout_one, partner, n):
    bf16 = jnp.bfloat16
    tiles = own_blocks.size // (16 * BLK)
    high = moments.astype(bf16)
    low = (moments - high.astype(jnp.float32)).astype(bf16)
    flat_layout = layout_one.reshape(-1)
    lay_tile = jnp.pad(flat_layout, (0, 16 * BLK - flat_layout.size)).astype(bf16)
    count = 3 * tiles + 1
    padded = -(-count // n) * n
    state = jnp.concatenate(
        [
            own_blocks.reshape(tiles, 16, BLK),
            high.reshape(tiles, 16, BLK),
            low.reshape(tiles, 16, BLK),
            lay_tile.reshape(1, 16, BLK),
            jnp.zeros((padded - count, 16, BLK), bf16),
        ]
    ).reshape(n, -1, BLK)
    spread = lax.all_to_all(state, "expert", split_axis=0, concat_axis=0, tiled=True)
    moved = lax.all_to_all(spread[partner], "expert", split_axis=0, concat_axis=0, tiled=True)
    moved = moved.reshape(padded, 16, BLK)
    new_blocks = moved[:tiles].reshape(own_blocks.shape)
    new_moments = (
        moved[tiles : 2 * tiles].astype(jnp.float32)
        + moved[2 * tiles : 3 * tiles].astype(jnp.float32)
    ).reshape(moments.shape)
    new_layout = (
        moved[3 * tiles].reshape(-1)[: flat_layout.size].astype(jnp.int32).reshape(layout_one.shape)
    )
    return new_blocks, new_moments, new_layout


def body(tokens, out_grad, expert_ids, route_weights, blocks, layout, moments, partner):
    f32, bf16 = jnp.float32, jnp.bfloat16
    n = lax.axis_size("expert")
    n_dp = lax.axis_size("dp")
    count, width = tokens.shape
    share = BLK // n_dp
    own = lax.dynamic_slice_in_dim(blocks[0], lax.axis_index("dp") * share, share, 2)
    own, old_moment, layout_one = move_state(own, moments[0], layout[0], partner, n)
    mats = lax.all_gather(own, "dp", axis=2, tiled=True)

    picks = expert_ids[None] == partner[:, None, None]
    named = jnp.any(picks, axis=2)
    before = jnp.tril(jnp.ones((count, count), bf16), -1)
    rank = dot(named.astype(bf16), before, NT)
    weight = jnp.sum(jnp.where(picks, route_weights[None].astype(f32), 0.0), axis=2)
    z, j, _, _ = peers()
    slot = jnp.where(named, rank + (z * CAP).astype(f32), -1.0)

    def by_plane(a):
        return a.reshape(NX, NZ, NCORE, count).transpose(1, 0, 2, 3).reshape(NZ, PLANE, count)

    meta = jnp.concatenate([by_plane(slot), by_plane(weight)], axis=1).astype(bf16)
    xs, choose = dispatch(tokens, out_grad, meta, 8)
    pg, sc, wg = expert_compute(layout_one, j.reshape(1), xs, mats, 448)
    token_grad, score = give_back(pg, sc, choose, count)
    score = score.reshape(NZ, NX, NCORE, count).transpose(1, 0, 2, 3).reshape(n, count)
    score = jnp.sum(jnp.where(picks, score[:, :, None], 0.0), axis=0)
    route_grad = (score / route_weights.astype(f32)).astype(bf16)

    shard = lax.psum_scatter(wg, "dp", scatter_dimension=2, tiled=True)
    moment = DECAY * old_moment + shard
    updated = (own.astype(f32) - RATE * moment).astype(bf16)
    gathered = lax.all_gather(updated, "dp", axis=2, tiled=True)
    return token_grad, route_grad, gathered[None], moment[None]


def solution(mesh):
    rows = P(("dp", "expert"), None)
    state = P("expert", None, None, None, None)
    moment = P("expert", None, None, "dp", None)
    return jax.shard_map(
        body,
        mesh=mesh,
        in_specs=(rows, rows, rows, rows, state, P("expert", None, None, None), moment, P()),
        out_specs=(rows, rows, state, moment),
        check_vma=False,
    )
```

```python
import functools

import jax
import jax.numpy as jnp
from jax import lax
from jax.experimental import pallas as pl
from jax.experimental.pallas import tpu as pltpu
from jax.sharding import PartitionSpec as P

HID = 1408
BLK = 128
CAP = 14
DECAY = 0.9
RATE = 0.01

NT = (((1,), (1,)), ((), ()))
TN = (((0,), (0,)), ((), ()))


def dot(a, b, dims=(((1,), (0,)), ((), ()))):
    return lax.dot_general(a, b, dims, preferred_element_type=jnp.float32)


def lanes(i):
    return pl.ds(pl.multiple_of(i * BLK, BLK), BLK)


def expert_kernel(lay, place_ref, x_ref, s_ref, w_ref, pg_ref, sc_ref, out_ref, wg_ref, gate, up, hg, hid, gg, ug, acc):
    nb = w_ref.shape[1]
    rows = x_ref.shape[1]
    per = x_ref.shape[2] // BLK

    def chunk(ref, i):
        return ref[i // per, :, lanes(i % per)]

    @pl.when(pl.program_id(0) == 0)
    def _():
        wg_ref[...] = jnp.zeros_like(wg_ref)

    gate[...] = jnp.zeros_like(gate)
    up[...] = jnp.zeros_like(up)
    hg[...] = jnp.zeros_like(hg)

    def first(b, carry):
        gate[:, lanes(lay[0, b, 1])] += dot(chunk(x_ref, lay[0, b, 0]), w_ref[0, b])
        up[:, lanes(lay[1, b, 1])] += dot(chunk(x_ref, lay[1, b, 0]), w_ref[1, b])
        hg[:, lanes(lay[2, b, 0])] += dot(chunk(s_ref, lay[2, b, 1]), w_ref[2, b], NT)
        return carry

    lax.fori_loop(0, nb, first, 0)

    def middle(j, score):
        g = gate[:, lanes(j)]
        u = up[:, lanes(j)]
        h = hg[:, lanes(j)]
        sig = jax.nn.sigmoid(g)
        act = g * sig
        hb = (act * u).astype(jnp.bfloat16)
        hid[:, lanes(j)] = hb
        gg[:, lanes(j)] = (h * u * sig * (1.0 + g * (1.0 - sig))).astype(jnp.bfloat16)
        ug[:, lanes(j)] = (h * act).astype(jnp.bfloat16)
        return score + hb.astype(jnp.float32) * h

    score = lax.fori_loop(0, HID // BLK, middle, jnp.zeros((rows, BLK), jnp.float32))
    total = jnp.sum(score, axis=1, keepdims=True)
    high = total.astype(jnp.bfloat16).astype(jnp.float32)
    lane = lax.broadcasted_iota(jnp.int32, (rows, BLK), 1)
    group = pl.program_id(0) * (rows // (NCORE * ROWS))
    for k in range(1, rows // (NCORE * ROWS)):
        group = group + (lax.broadcasted_iota(jnp.int32, (rows, BLK), 0) >= k * NCORE * ROWS).astype(jnp.int32)
    place = jnp.where(group == 0, 0, NX - group) * NCORE + place_ref[0]
    sc_ref[...] = jnp.where(
        lane == place, high, jnp.where(lane == place + 8, total - high, 0.0)
    ).astype(jnp.bfloat16)

    acc[...] = jnp.zeros_like(acc)

    def last(b, carry):
        r0, c0, r1, c1 = lay[0, b, 0], lay[0, b, 1], lay[1, b, 0], lay[1, b, 1]
        acc[:, lanes(r0)] += dot(gg[:, lanes(c0)], w_ref[0, b], NT)
        acc[:, lanes(r1)] += dot(ug[:, lanes(c1)], w_ref[1, b], NT)
        wg_ref[0, b] += dot(chunk(x_ref, r0), gg[:, lanes(c0)], TN)
        wg_ref[1, b] += dot(chunk(x_ref, r1), ug[:, lanes(c1)], TN)
        wg_ref[2, b] += dot(hid[:, lanes(lay[2, b, 0])], chunk(s_ref, lay[2, b, 1]), TN)
        return carry

    lax.fori_loop(0, nb, last, 0)
    for q in range(pg_ref.shape[0]):
        width = pg_ref.shape[2]
        pg_ref[q] = acc[:, q * width : (q + 1) * width].astype(jnp.bfloat16)

    @pl.when(pl.program_id(0) == pl.num_programs(0) - 1)
    def _():
        share = out_ref.shape[2]
        for y in range(out_ref.shape[0]):
            for m in range(w_ref.shape[0]):
                out_ref[y, m * nb : (m + 1) * nb] = wg_ref[m, :, y * share : (y + 1) * share, :].astype(jnp.bfloat16)


def expert_compute(layout_one, place, xs, mats, tile):
    nq, rows, width = xs.shape
    nq = nq // 2
    nm, nb = mats.shape[:2]
    row_spec = pl.BlockSpec((nq, tile, width), lambda i, lay, place: (0, i, 0))
    grad_spec = pl.BlockSpec((nq, tile, width), lambda i, lay, place: (1, i, 0))
    f32, bf16 = jnp.float32, jnp.bfloat16
    return pl.pallas_call(
        expert_kernel,
        grid_spec=pltpu.PrefetchScalarGridSpec(
            num_scalar_prefetch=2,
            grid=(rows // tile,),
            in_specs=[
                row_spec,
                grad_spec,
                pl.BlockSpec((nm, nb, BLK, BLK), lambda i, lay, place: (0, 0, 0, 0)),
            ],
            out_specs=[
                row_spec,
                pl.BlockSpec((tile, BLK), lambda i, lay, place: (i, 0)),
                pl.BlockSpec((NY, nm * nb, BLK // NY, BLK), lambda i, lay, place: (0, 0, 0, 0)),
            ],
            scratch_shapes=[
                pltpu.VMEM(mats.shape, f32),
                pltpu.VMEM((tile, HID), f32),
                pltpu.VMEM((tile, HID), f32),
                pltpu.VMEM((tile, HID), f32),
                pltpu.VMEM((tile, HID), bf16),
                pltpu.VMEM((tile, HID), bf16),
                pltpu.VMEM((tile, HID), bf16),
                pltpu.VMEM((tile, nq * width), f32),
            ],
        ),
        out_shape=[
            jax.ShapeDtypeStruct((nq, rows, width), bf16),
            jax.ShapeDtypeStruct((rows, BLK), bf16),
            jax.ShapeDtypeStruct((NY, nm * nb, BLK // NY, BLK), bf16),
        ],
        compiler_params=pltpu.CompilerParams(vmem_limit_bytes=56 << 20),
        cost_estimate=pl.CostEstimate(
            flops=8 * nb * rows * BLK * BLK * 2,
            bytes_accessed=3 * xs.size + mats.size * 6,
            transcendentals=rows * HID,
        ),
    )(layout_one, place, xs, xs, mats)


NX, NZ, NCORE, NY = 4, 8, 2, 8
PLANE = NX * NCORE
ROWS = NZ * CAP
MESH = pl.DeviceIdType.MESH


class Place:
    def __init__(self):
        me = lax.axis_index("expert")
        self.y = lax.axis_index("dp")
        self.me = me
        self.x = me // (NZ * NCORE)
        self.z = (me // NCORE) % NZ
        self.core = me % NCORE

    def along(self, dz):
        return (self.y, self.x * (NZ * NCORE) + (self.z + dz) % NZ * NCORE + self.core)

    def across(self, dx, core):
        return (self.y, (self.x + dx) % NX * (NZ * NCORE) + self.z * NCORE + core)

    def over(self, dy):
        return ((self.y + dy) % NY, self.me)

    def meet(self, with_y):
        others = [self.along(k) for k in range(1, NZ)]
        others += [self.across(dx, c) for dx in range(1, NX) for c in range(NCORE)]
        others.append(self.across(0, 1 - self.core))
        if with_y:
            others += [self.over(k) for k in range(1, NY)]
        barrier = pltpu.get_barrier_semaphore()
        for other in others:
            pl.semaphore_signal(barrier, inc=1, device_id=other, device_id_type=MESH)
        pl.semaphore_wait(barrier, len(others))


def send(src, dst, send_sem, recv_sem, device):
    return pltpu.make_async_remote_copy(
        src_ref=src,
        dst_ref=dst,
        send_sem=send_sem,
        recv_sem=recv_sem,
        device_id=device,
        device_id_type=MESH,
    )


def span(i, size):
    return pl.ds(pl.multiple_of(i * size, size), size)


class Exchange:
    far = NX // 2

    def __init__(self, place, src, dst, relay, own_sem, send_sem, recv_sem, relay_send, relay_recv):
        self.place, self.src, self.dst, self.relay = place, src, dst, relay
        self.own_sem, self.send_sem, self.recv_sem = own_sem, send_sem, recv_sem
        self.relay_send, self.relay_recv = relay_send, relay_recv

    def direct(self, q, dx, core):
        number = dx * NCORE + core
        landing = (NX - dx) % NX * NCORE + self.place.core
        return send(
            self.src.at[q, span(number, ROWS)],
            self.dst.at[q, span(landing, ROWS)],
            self.send_sem.at[q, number],
            self.recv_sem.at[q, landing],
            self.place.across(dx, core),
        )

    def first_leg(self, q, way):
        number = self.far * NCORE + way
        return send(
            self.src.at[q, span(number, ROWS)],
            self.relay.at[q, way],
            self.send_sem.at[q, number],
            self.relay_recv.at[q, way],
            self.place.across(1 if way == 0 else NX - 1, self.place.core),
        )

    def second_leg(self, q, way):
        landing = self.far * NCORE + self.place.core
        return send(
            self.relay.at[q, way],
            self.dst.at[q, span(landing, ROWS)],
            self.relay_send.at[q, way],
            self.recv_sem.at[q, landing],
            self.place.across(1 if way == 0 else NX - 1, way),
        )

    def own(self, q):
        rows = span(self.place.core, ROWS)
        return pltpu.make_async_copy(self.src.at[q, rows], self.dst.at[q, rows], self.own_sem.at[q])

    def start(self, q, steps=(2, 1, 3, 0)):
        for dx in steps:
            if dx == 0:
                self.direct(q, 0, 1 - self.place.core).start()
                self.own(q).start()
            elif dx == self.far and self.relay is not None:
                for way in range(2):
                    self.first_leg(q, way).start()
            else:
                for core in range(NCORE):
                    self.direct(q, dx, core).start()

    def forward(self, q):
        for way in range(2):
            self.first_leg(q, way).wait_recv()
            self.second_leg(q, way).start()

    def arrive(self, q):
        def one(landing):
            part = self.dst.at[q, span(landing, ROWS)]
            send(part, part, self.send_sem.at[q, landing], self.recv_sem.at[q, landing], self.place.across(1, 0)).wait_recv()

        for dx in range(1, NX):
            for core in range(NCORE):
                one(dx * NCORE + core)
        one(1 - self.place.core)
        self.own(q).wait()

    def leave(self, q):
        for dx in range(1, NX):
            for core in range(NCORE):
                if dx == self.far and self.relay is not None:
                    self.first_leg(q, core).wait_send()
                    self.second_leg(q, core).wait_send()
                else:
                    self.direct(q, dx, core).wait_send()
        self.direct(q, 0, 1 - self.place.core).wait_send()


def dispatch_kernel(
    tok, og, meta, xs, chosen, ring, picked, choose, notes, relay,
    own_sem, notes_send, notes_recv, ring_send, ring_recv, out_own, out_send, out_recv, relay_send, relay_recv, keep_sem,
):
    count = tok.shape[0]
    chunks, _, width = ring.shape
    half = chunks // 2
    place = Place()
    z = place.z
    out = Exchange(place, picked, xs, relay, out_own, out_send, out_recv, relay_send, relay_recv)

    def own_copy(q):
        src = tok if q < half else og
        return pltpu.make_async_copy(
            src.at[:, (q % half) * width : (q % half + 1) * width],
            ring.at[q, span(z, count)],
            own_sem.at[q],
        )

    for q in range(chunks):
        own_copy(q).start()
    own_notes = pltpu.make_async_copy(meta.at[z], notes.at[z], keep_sem.at[1])
    own_notes.start()
    place.meet(False)

    def note(k, source):
        return send(
            meta.at[(z + k) % NZ], notes.at[source], notes_send.at[k], notes_recv.at[k], place.along(k)
        )

    for k in range(1, NZ):
        note(k, z).start()
    for q in range(chunks):
        own_copy(q).wait()
    own_notes.wait()

    def hop(q, way, step, arriving):
        rows = count
        if way == 0:
            source = (z + 2 * NZ - step - (1 if arriving else 0)) % NZ
        else:
            source = (z + step + (1 if arriving else 0)) % NZ
        start = source * count
        if step == NZ // 2 - 1:
            rows = count // 2
            start = start + way * rows
        block = ring.at[q, pl.ds(pl.multiple_of(start, rows), rows)]
        return send(
            block,
            block,
            ring_send.at[q, way, step],
            ring_recv.at[q, way, step],
            place.along(1 if way == 0 else NZ - 1),
        )

    def keep():
        return pltpu.make_async_copy(choose.at[0], chosen, keep_sem.at[0])

    def build():
        for k in range(1, NZ):
            note(k, (z + NZ - k) % NZ).wait_recv()
        row = lax.broadcasted_iota(jnp.int32, (ROWS, count), 0).astype(jnp.float32)

        def fill(source, carry):
            both = notes[source].astype(jnp.float32)
            for other in range(PLANE):
                hit = row == both[other : other + 1, :]
                rows = slice(other * ROWS, (other + 1) * ROWS)
                scale = both[PLANE + other : PLANE + other + 1, :]
                choose[0, rows, span(source, count)] = jnp.where(hit, 1.0, 0.0).astype(jnp.bfloat16)
                choose[1, rows, span(source, count)] = jnp.where(hit, scale, 0.0).astype(jnp.bfloat16)
            return carry

        lax.fori_loop(0, NZ, fill, 0)
        keep().start()

    def step(i, carry):
        for s in range(NZ // 2):
            q = i - s

            @pl.when((q >= 0) & (q < chunks))
            def _():
                for way in range(2):
                    if s:
                        hop(q, way, s - 1, True).wait_recv()
                    hop(q, way, s, False).start()

        pl.when(i == 1)(build)

        @pl.when((i > NZ // 2) & (i <= NZ // 2 + chunks))
        def _():
            out.forward(i - NZ // 2 - 1)

        q = i - NZ // 2

        @pl.when((q >= 0) & (q < chunks))
        def _():
            for way in range(2):
                hop(q, way, NZ // 2 - 1, True).wait_recv()
            for h in (1, 0):
                rows = slice(h * (PLANE // 2) * ROWS, (h + 1) * (PLANE // 2) * ROWS)
                picked[q, rows, :] = dot(choose[q // half, rows, :], ring[q]).astype(jnp.bfloat16)
                out.start(q, (2, 3) if h else (1, 0))

        return carry

    lax.fori_loop(0, chunks + NZ // 2 + 1, step, 0)

    def finish(q, carry):
        for way in range(2):
            for s in range(NZ // 2):
                hop(q, way, s, False).wait_send()
        out.leave(q)
        out.arrive(q)
        return carry

    lax.fori_loop(0, chunks, finish, 0)
    for k in range(1, NZ):
        note(k, z).wait_send()
    keep().wait()


def dispatch(tokens, grads, meta, chunks):
    count, features = tokens.shape
    width = 2 * features // chunks
    bf16 = jnp.bfloat16
    slots = PLANE * ROWS
    dma = pltpu.SemaphoreType.DMA
    anywhere = pl.BlockSpec(memory_space=pl.ANY)
    return pl.pallas_call(
        dispatch_kernel,
        in_specs=[anywhere, anywhere, anywhere],
        out_specs=[anywhere, anywhere],
        out_shape=[
            jax.ShapeDtypeStruct((chunks, slots, width), bf16),
            jax.ShapeDtypeStruct((slots, NZ * count), bf16),
        ],
        scratch_shapes=[
            pltpu.VMEM((chunks, NZ * count, width), bf16),
            pltpu.VMEM((chunks, slots, width), bf16),
            pltpu.VMEM((2, slots, NZ * count), bf16),
            pltpu.VMEM(meta.shape, bf16),
            pltpu.VMEM((chunks, 2, ROWS, width), bf16),
            dma((chunks,)),
            dma((NZ,)),
            dma((NZ,)),
            dma((chunks, 2, NZ // 2)),
            dma((chunks, 2, NZ // 2)),
            dma((chunks,)),
            dma((chunks, PLANE)),
            dma((chunks, PLANE)),
            dma((chunks, 2)),
            dma((chunks, 2)),
            dma((2,)),
        ],
        compiler_params=pltpu.CompilerParams(
            collective_id=0, has_side_effects=True, vmem_limit_bytes=56 << 20
        ),
        cost_estimate=pl.CostEstimate(
            flops=2 * slots * NZ * count * 2 * features, bytes_accessed=300 << 20, transcendentals=0
        ),
    )(tokens, grads, meta)


def return_kernel(
    pg, sc, choose, wg, own_blocks, old_moment, tg, score, moment, blocks,
    back, marks, relay, part, leaving, landed, sums, grads,
    x_own, x_send, x_recv, relay_send, relay_recv, mark_own, mark_send, mark_recv,
    z_send, z_recv, sum_send, sum_recv, y_send, y_recv, share_send, share_recv,
):
    chunks, slots, width = pg.shape
    count = tg.shape[0]
    last = NZ // 2 - 1
    place = Place()
    z, y = place.z, place.y
    cross = Exchange(place, pg, back, relay, x_own, x_send, x_recv, relay_send, relay_recv)
    mark = Exchange(place, sc, marks, None, mark_own, mark_send, mark_recv, None, None)

    own_grads = pltpu.make_async_copy(wg.at[y], grads.at[y], y_send.at[0])
    own_grads.start()
    place.meet(True)
    cross.start(0)

    def grad(k, landing):
        return send(wg.at[(y + k) % NY], grads.at[landing], y_send.at[k], y_recv.at[k], place.over(k))

    for k in range(1, NY):
        grad(k, y).start()
    mark.start(0)
    cross.start(1)
    cross.forward(0)

    def share(way, step, arriving):
        if way == 0:
            source = (y + 2 * NY - step - (1 if arriving else 0)) % NY
        else:
            source = (y + step + (1 if arriving else 0)) % NY
        n = blocks.shape[0]
        which = slice(0, n)
        if step == NY // 2 - 1:
            which = slice(way * (n // 2), (way + 1) * (n // 2))
        rows = blocks.at[which, span(source, BLK // NY)]
        return send(
            rows, rows, share_send.at[way, step], share_recv.at[way, step], place.over(1 if way == 0 else NY - 1)
        )

    def update():
        for k in range(1, NY):
            grad(k, (y + NY - k) % NY).wait_recv()
        own_grads.wait()

        def one(b, carry):
            total = DECAY * old_moment[b]
            for source in range(NY):
                total = total + grads[source, b].astype(jnp.float32)
            moment[b] = total
            fresh = own_blocks[b].astype(jnp.float32) - RATE * total
            blocks[b, span(y, BLK // NY), :] = fresh.astype(jnp.bfloat16)
            return carry

        lax.fori_loop(0, blocks.shape[0], one, 0)
        for way in range(2):
            share(way, 0, False).start()

    def hop(q, way, step):
        rows = slice(0, count)
        if step == 0:
            rows = slice(way * (count // 2), (way + 1) * (count // 2))
        return send(
            leaving.at[q, way, step, rows],
            landed.at[q, way, step, rows],
            z_send.at[q, way, step],
            z_recv.at[q, way, step],
            place.along(1 if way == 0 else NZ - 1),
        )

    def target(way, step):
        if way == 0:
            return (z + NZ // 2 - step) % NZ
        return (z + NZ // 2 + step) % NZ

    def own_sum():
        return pltpu.make_async_copy(sums.at[z], score.at[z], sum_send.at[0])

    def summed(k, landing):
        return send(sums.at[(z + k) % NZ], score.at[landing], sum_send.at[k], sum_recv.at[k], place.along(k))

    def step(i, carry):
        @pl.when(i < chunks)
        def _():
            q = i
            cross.arrive(q)

            def add(t, carry):
                cols = span(t, 2 * count)
                part[q, cols, :] = dot(choose[:, cols], back[q], TN)
                return carry

            lax.fori_loop(0, NZ // 2, add, 0)
            for way in range(2):
                size = count // 2
                start = target(way, 0) * count + way * size
                rows = pl.ds(pl.multiple_of(start, size), size)
                leaving[q, way, 0, way * size : (way + 1) * size, :] = part[q, rows, :].astype(jnp.bfloat16)
                hop(q, way, 0).start()

        for s in range(1, NZ // 2):
            q = i - s

            @pl.when((q >= 0) & (q < chunks))
            def _():
                for way in range(2):
                    hop(q, way, s - 1).wait_recv()
                    mine = part[q, span(target(way, s), count), :]
                    if s == 1:
                        size = count // 2
                        near = slice(way * size, (way + 1) * size)
                        far = slice((1 - way) * size, (2 - way) * size)
                        more = landed[q, way, 0, near, :].astype(jnp.float32)
                        leaving[q, way, 1, near, :] = (mine[near] + more).astype(jnp.bfloat16)
                        leaving[q, way, 1, far, :] = mine[far].astype(jnp.bfloat16)
                    else:
                        more = landed[q, way, s - 1].astype(jnp.float32)
                        leaving[q, way, s] = (mine + more).astype(jnp.bfloat16)
                    hop(q, way, s).start()

        q = i - NZ // 2

        @pl.when(q >= 0)
        def _():
            total = part[q, span(z, count), :]
            for way in range(2):
                hop(q, way, last).wait_recv()
                total = total + landed[q, way, last].astype(jnp.float32)
            tg[:, pl.ds(pl.multiple_of(q * width, width), width)] = total.astype(jnp.bfloat16)

        @pl.when(i + 2 < chunks)
        def _():
            cross.start(i + 2)

        @pl.when(i + 1 < chunks)
        def _():
            cross.forward(i + 1)

        pl.when(i == 2)(update)
        for s in range(1, NY // 2):

            @pl.when(i == 2 + s)
            def _():
                for way in range(2):
                    share(way, s - 1, True).wait_recv()
                    share(way, s, False).start()

        @pl.when(i == chunks - 1)
        def _():
            mark.arrive(0)
            spread = dot(marks[0], choose[...], TN)
            both = spread[:PLANE] + spread[PLANE : 2 * PLANE]
            for source in range(NZ):
                sums[source] = both[:, source * count : (source + 1) * count]
            own_sum().start()
            for k in range(1, NZ):
                summed(k, z).start()

        return carry

    lax.fori_loop(0, chunks + NZ // 2, step, 0)

    def finish(q, carry):
        cross.leave(q)
        for way in range(2):
            for s in range(NZ // 2):
                hop(q, way, s).wait_send()
        return carry

    lax.fori_loop(0, chunks, finish, 0)
    mark.leave(0)
    own_sum().wait()
    for k in range(1, NZ):
        summed(k, z).wait_send()
        summed(k, (z + NZ - k) % NZ).wait_recv()
    for k in range(1, NY):
        grad(k, y).wait_send()
    for way in range(2):
        share(way, NY // 2 - 1, True).wait_recv()
        for s in range(NY // 2):
            share(way, s, False).wait_send()


def give_back(pg, sc, choose, wg, own_blocks, old_moment, count):
    chunks, slots, width = pg.shape
    f32, bf16 = jnp.float32, jnp.bfloat16
    dma = pltpu.SemaphoreType.DMA
    anywhere = pl.BlockSpec(memory_space=pl.ANY)
    vmem = pl.BlockSpec(memory_space=pltpu.VMEM)
    return pl.pallas_call(
        return_kernel,
        in_specs=[anywhere, anywhere, vmem, anywhere, vmem, vmem],
        out_specs=[vmem, anywhere, vmem, vmem],
        out_shape=[
            jax.ShapeDtypeStruct((count, chunks * width), bf16),
            jax.ShapeDtypeStruct((NZ, PLANE, count), f32),
            jax.ShapeDtypeStruct(old_moment.shape, f32),
            jax.ShapeDtypeStruct((wg.shape[1], BLK, BLK), bf16),
        ],
        scratch_shapes=[
            pltpu.VMEM((chunks, slots, width), bf16),
            pltpu.VMEM(sc.shape, bf16),
            pltpu.VMEM((chunks, 2, ROWS, width), bf16),
            pltpu.VMEM((chunks, NZ * count, width), f32),
            pltpu.VMEM((chunks, 2, NZ // 2, count, width), bf16),
            pltpu.VMEM((chunks, 2, NZ // 2, count, width), bf16),
            pltpu.VMEM((NZ, PLANE, count), f32),
            pltpu.VMEM(wg.shape, bf16),
            dma((chunks,)),
            dma((chunks, PLANE)),
            dma((chunks, PLANE)),
            dma((chunks, 2)),
            dma((chunks, 2)),
            dma((1,)),
            dma((1, PLANE)),
            dma((1, PLANE)),
            dma((chunks, 2, NZ // 2)),
            dma((chunks, 2, NZ // 2)),
            dma((NZ,)),
            dma((NZ,)),
            dma((NY,)),
            dma((NY,)),
            dma((2, NY // 2)),
            dma((2, NY // 2)),
        ],
        compiler_params=pltpu.CompilerParams(
            collective_id=1, has_side_effects=True, vmem_limit_bytes=56 << 20
        ),
        cost_estimate=pl.CostEstimate(
            flops=2 * slots * NZ * count * chunks * width, bytes_accessed=150 << 20, transcendentals=0
        ),
    )(pg, sc, choose, wg, own_blocks, old_moment)


def move_state(own_blocks, moments, layout_one, partner, n):
    bf16 = jnp.bfloat16
    tiles = own_blocks.size // (16 * BLK)
    high = moments.astype(bf16)
    low = (moments - high.astype(jnp.float32)).astype(bf16)
    flat_layout = layout_one.reshape(-1)
    lay_tile = jnp.pad(flat_layout, (0, 16 * BLK - flat_layout.size)).astype(bf16)
    count = 3 * tiles + 1
    padded = -(-count // n) * n
    state = jnp.concatenate(
        [
            own_blocks.reshape(tiles, 16, BLK),
            high.reshape(tiles, 16, BLK),
            low.reshape(tiles, 16, BLK),
            lay_tile.reshape(1, 16, BLK),
            jnp.zeros((padded - count, 16, BLK), bf16),
        ]
    ).reshape(n, -1, BLK)
    spread = lax.all_to_all(state, "expert", split_axis=0, concat_axis=0, tiled=True)
    moved = lax.all_to_all(spread[partner], "expert", split_axis=0, concat_axis=0, tiled=True)
    moved = moved.reshape(padded, 16, BLK)
    new_blocks = moved[:tiles].reshape(own_blocks.shape)
    new_moments = (
        moved[tiles : 2 * tiles].astype(jnp.float32)
        + moved[2 * tiles : 3 * tiles].astype(jnp.float32)
    ).reshape(moments.shape)
    new_layout = (
        moved[3 * tiles].reshape(-1)[: flat_layout.size].astype(jnp.int32).reshape(layout_one.shape)
    )
    return new_blocks, new_moments, new_layout


def body(tokens, out_grad, expert_ids, route_weights, blocks, layout, moments, partner):
    f32, bf16 = jnp.float32, jnp.bfloat16
    n = lax.axis_size("expert")
    n_dp = lax.axis_size("dp")
    count, width = tokens.shape
    share = BLK // n_dp
    own = lax.dynamic_slice_in_dim(blocks[0], lax.axis_index("dp") * share, share, 2)
    own, old_moment, layout_one = move_state(own, moments[0], layout[0], partner, n)
    mats = lax.all_gather(own, "dp", axis=2, tiled=True)

    place = Place()
    number = jnp.arange(n, dtype=jnp.int32)
    where = (place.x + number // NCORE % NX) % NX * (NZ * NCORE) + number // PLANE * NCORE + number % NCORE
    holds = partner[where]
    picks = expert_ids[None] == holds[:, None, None]
    named = jnp.any(picks, axis=2)
    before = jnp.tril(jnp.ones((count, count), bf16), -1)
    rank = dot(named.astype(bf16), before, NT)
    weight = jnp.sum(jnp.where(picks, route_weights[None].astype(f32), 0.0), axis=2)
    slot = jnp.where(named, rank + (place.z * CAP).astype(f32), -1.0)
    meta = jnp.concatenate(
        [slot.reshape(NZ, PLANE, count), weight.reshape(NZ, PLANE, count)], axis=1
    ).astype(bf16)
    xs, choose = dispatch(tokens, out_grad, meta, 8)
    pg, sc, wg = expert_compute(layout_one, place.core.reshape(1), xs, mats, 448)
    tiles = own.shape[0] * own.shape[1]
    token_grad, score, moment, updated = give_back(
        pg, sc[None], choose, wg, own.reshape(tiles, share, BLK), old_moment.reshape(tiles, share, BLK), count
    )
    score = jnp.sum(jnp.where(picks, score.reshape(n, count)[:, :, None], 0.0), axis=0)
    route_grad = (score / route_weights.astype(f32)).astype(bf16)
    return (
        token_grad,
        route_grad,
        updated.reshape(blocks.shape),
        moment.reshape(moments.shape),
    )


def solution(mesh):
    rows = P(("dp", "expert"), None)
    state = P("expert", None, None, None, None)
    moment = P("expert", None, None, "dp", None)
    return jax.shard_map(
        body,
        mesh=mesh,
        in_specs=(rows, rows, rows, rows, state, P("expert", None, None, None), moment, P()),
        out_specs=(rows, rows, state, moment),
        check_vma=False,
    )
```

```python
import functools

import jax
import jax.numpy as jnp
from jax import lax
from jax.experimental import pallas as pl
from jax.experimental.pallas import tpu as pltpu
from jax.sharding import PartitionSpec as P

HID = 1408
BLK = 128
CAP = 14
DECAY = 0.9
RATE = 0.01

NT = (((1,), (1,)), ((), ()))
TN = (((0,), (0,)), ((), ()))


def dot(a, b, dims=(((1,), (0,)), ((), ()))):
    return lax.dot_general(a, b, dims, preferred_element_type=jnp.float32)


def lanes(i):
    return pl.ds(pl.multiple_of(i * BLK, BLK), BLK)


def expert_kernel(lay, place_ref, x_ref, s_ref, w_ref, pg_ref, sc_ref, out_ref, wg_ref, gate, up, hg, hid, gg, ug, acc):
    nb = w_ref.shape[1]
    rows = x_ref.shape[1]
    per = x_ref.shape[2] // BLK

    def chunk(ref, i):
        return ref[i // per, :, lanes(i % per)]

    @pl.when(pl.program_id(0) == 0)
    def _():
        wg_ref[...] = jnp.zeros_like(wg_ref)

    gate[...] = jnp.zeros_like(gate)
    up[...] = jnp.zeros_like(up)
    hg[...] = jnp.zeros_like(hg)

    def first(b, carry):
        gate[:, lanes(lay[0, b, 1])] += dot(chunk(x_ref, lay[0, b, 0]), w_ref[0, b])
        up[:, lanes(lay[1, b, 1])] += dot(chunk(x_ref, lay[1, b, 0]), w_ref[1, b])
        hg[:, lanes(lay[2, b, 0])] += dot(chunk(s_ref, lay[2, b, 1]), w_ref[2, b], NT)
        return carry

    lax.fori_loop(0, nb, first, 0)

    def middle(j, score):
        g = gate[:, lanes(j)]
        u = up[:, lanes(j)]
        h = hg[:, lanes(j)]
        sig = jax.nn.sigmoid(g)
        act = g * sig
        hb = (act * u).astype(jnp.bfloat16)
        hid[:, lanes(j)] = hb
        gg[:, lanes(j)] = (h * u * sig * (1.0 + g * (1.0 - sig))).astype(jnp.bfloat16)
        ug[:, lanes(j)] = (h * act).astype(jnp.bfloat16)
        return score + hb.astype(jnp.float32) * h

    score = lax.fori_loop(0, HID // BLK, middle, jnp.zeros((rows, BLK), jnp.float32))
    total = jnp.sum(score, axis=1, keepdims=True)
    high = total.astype(jnp.bfloat16).astype(jnp.float32)
    lane = lax.broadcasted_iota(jnp.int32, (rows, BLK), 1)
    group = pl.program_id(0) * (rows // (NCORE * ROWS))
    for k in range(1, rows // (NCORE * ROWS)):
        group = group + (lax.broadcasted_iota(jnp.int32, (rows, BLK), 0) >= k * NCORE * ROWS).astype(jnp.int32)
    place = jnp.where(group == 0, 0, NX - group) * NCORE + place_ref[0]
    sc_ref[...] = jnp.where(
        lane == place, high, jnp.where(lane == place + 8, total - high, 0.0)
    ).astype(jnp.bfloat16)

    acc[...] = jnp.zeros_like(acc)

    def last(b, carry):
        r0, c0, r1, c1 = lay[0, b, 0], lay[0, b, 1], lay[1, b, 0], lay[1, b, 1]
        acc[:, lanes(r0)] += dot(gg[:, lanes(c0)], w_ref[0, b], NT)
        acc[:, lanes(r1)] += dot(ug[:, lanes(c1)], w_ref[1, b], NT)
        wg_ref[0, b] += dot(chunk(x_ref, r0), gg[:, lanes(c0)], TN)
        wg_ref[1, b] += dot(chunk(x_ref, r1), ug[:, lanes(c1)], TN)
        wg_ref[2, b] += dot(hid[:, lanes(lay[2, b, 0])], chunk(s_ref, lay[2, b, 1]), TN)
        return carry

    lax.fori_loop(0, nb, last, 0)
    for q in range(pg_ref.shape[0]):
        width = pg_ref.shape[2]
        pg_ref[q] = acc[:, q * width : (q + 1) * width].astype(jnp.bfloat16)

    @pl.when(pl.program_id(0) == pl.num_programs(0) - 1)
    def _():
        share = out_ref.shape[2]
        for y in range(out_ref.shape[0]):
            for m in range(w_ref.shape[0]):
                out_ref[y, m * nb : (m + 1) * nb] = wg_ref[m, :, y * share : (y + 1) * share, :].astype(jnp.bfloat16)


def expert_compute(layout_one, place, xs, mats, tile):
    nq, rows, width = xs.shape
    nq = nq // 2
    nm, nb = mats.shape[:2]
    row_spec = pl.BlockSpec((nq, tile, width), lambda i, lay, place: (0, i, 0))
    grad_spec = pl.BlockSpec((nq, tile, width), lambda i, lay, place: (1, i, 0))
    f32, bf16 = jnp.float32, jnp.bfloat16
    return pl.pallas_call(
        expert_kernel,
        grid_spec=pltpu.PrefetchScalarGridSpec(
            num_scalar_prefetch=2,
            grid=(rows // tile,),
            in_specs=[
                row_spec,
                grad_spec,
                pl.BlockSpec((nm, nb, BLK, BLK), lambda i, lay, place: (0, 0, 0, 0)),
            ],
            out_specs=[
                pl.BlockSpec((2 * nq, tile, width // 2), lambda i, lay, place: (0, i, 0)),
                pl.BlockSpec((tile, BLK), lambda i, lay, place: (i, 0)),
                pl.BlockSpec((NY, nm * nb, BLK // NY, BLK), lambda i, lay, place: (0, 0, 0, 0)),
            ],
            scratch_shapes=[
                pltpu.VMEM(mats.shape, f32),
                pltpu.VMEM((tile, HID), f32),
                pltpu.VMEM((tile, HID), f32),
                pltpu.VMEM((tile, HID), f32),
                pltpu.VMEM((tile, HID), bf16),
                pltpu.VMEM((tile, HID), bf16),
                pltpu.VMEM((tile, HID), bf16),
                pltpu.VMEM((tile, nq * width), f32),
            ],
        ),
        out_shape=[
            jax.ShapeDtypeStruct((2 * nq, rows, width // 2), bf16),
            jax.ShapeDtypeStruct((rows, BLK), bf16),
            jax.ShapeDtypeStruct((NY, nm * nb, BLK // NY, BLK), bf16),
        ],
        compiler_params=pltpu.CompilerParams(vmem_limit_bytes=56 << 20),
        cost_estimate=pl.CostEstimate(
            flops=8 * nb * rows * BLK * BLK * 2,
            bytes_accessed=3 * xs.size + mats.size * 6,
            transcendentals=rows * HID,
        ),
    )(layout_one, place, xs, xs, mats)


NX, NZ, NCORE, NY = 4, 8, 2, 8
PLANE = NX * NCORE
ROWS = NZ * CAP
MESH = pl.DeviceIdType.MESH


class Place:
    def __init__(self):
        me = lax.axis_index("expert")
        self.y = lax.axis_index("dp")
        self.me = me
        self.x = me // (NZ * NCORE)
        self.z = (me // NCORE) % NZ
        self.core = me % NCORE

    def along(self, dz):
        return (self.y, self.x * (NZ * NCORE) + (self.z + dz) % NZ * NCORE + self.core)

    def across(self, dx, core):
        return (self.y, (self.x + dx) % NX * (NZ * NCORE) + self.z * NCORE + core)

    def over(self, dy):
        return ((self.y + dy) % NY, self.me)

    def meet(self, with_y):
        others = [self.along(k) for k in range(1, NZ)]
        others += [self.across(dx, c) for dx in range(1, NX) for c in range(NCORE)]
        others.append(self.across(0, 1 - self.core))
        if with_y:
            others += [self.over(k) for k in range(1, NY)]
        barrier = pltpu.get_barrier_semaphore()
        for other in others:
            pl.semaphore_signal(barrier, inc=1, device_id=other, device_id_type=MESH)
        pl.semaphore_wait(barrier, len(others))


def send(src, dst, send_sem, recv_sem, device):
    return pltpu.make_async_remote_copy(
        src_ref=src,
        dst_ref=dst,
        send_sem=send_sem,
        recv_sem=recv_sem,
        device_id=device,
        device_id_type=MESH,
    )


def span(i, size):
    return pl.ds(pl.multiple_of(i * size, size), size)


class Exchange:
    far = NX // 2

    def __init__(self, place, src, dst, relay, own_sem, send_sem, recv_sem, relay_send, relay_recv):
        self.place, self.src, self.dst, self.relay = place, src, dst, relay
        self.own_sem, self.send_sem, self.recv_sem = own_sem, send_sem, recv_sem
        self.relay_send, self.relay_recv = relay_send, relay_recv

    def direct(self, q, dx, core):
        number = dx * NCORE + core
        landing = (NX - dx) % NX * NCORE + self.place.core
        return send(
            self.src.at[q, span(number, ROWS)],
            self.dst.at[q, span(landing, ROWS)],
            self.send_sem.at[q, number],
            self.recv_sem.at[q, landing],
            self.place.across(dx, core),
        )

    def first_leg(self, q, way):
        number = self.far * NCORE + way
        return send(
            self.src.at[q, span(number, ROWS)],
            self.relay.at[q, way],
            self.send_sem.at[q, number],
            self.relay_recv.at[q, way],
            self.place.across(1 if way == 0 else NX - 1, self.place.core),
        )

    def second_leg(self, q, way):
        landing = self.far * NCORE + self.place.core
        return send(
            self.relay.at[q, way],
            self.dst.at[q, span(landing, ROWS)],
            self.relay_send.at[q, way],
            self.recv_sem.at[q, landing],
            self.place.across(1 if way == 0 else NX - 1, way),
        )

    def own(self, q):
        rows = span(self.place.core, ROWS)
        return pltpu.make_async_copy(self.src.at[q, rows], self.dst.at[q, rows], self.own_sem.at[q])

    def start(self, q, steps=(2, 1, 3, 0)):
        for dx in steps:
            if dx == 0:
                self.direct(q, 0, 1 - self.place.core).start()
                self.own(q).start()
            elif dx == self.far and self.relay is not None:
                for way in range(2):
                    self.first_leg(q, way).start()
            else:
                for core in range(NCORE):
                    self.direct(q, dx, core).start()

    def forward(self, q):
        for way in range(2):
            self.first_leg(q, way).wait_recv()
            self.second_leg(q, way).start()

    def arrive(self, q):
        def one(landing):
            part = self.dst.at[q, span(landing, ROWS)]
            send(part, part, self.send_sem.at[q, landing], self.recv_sem.at[q, landing], self.place.across(1, 0)).wait_recv()

        for dx in range(1, NX):
            for core in range(NCORE):
                one(dx * NCORE + core)
        one(1 - self.place.core)
        self.own(q).wait()

    def leave(self, q):
        for dx in range(1, NX):
            for core in range(NCORE):
                if dx == self.far and self.relay is not None:
                    self.first_leg(q, core).wait_send()
                    self.second_leg(q, core).wait_send()
                else:
                    self.direct(q, dx, core).wait_send()
        self.direct(q, 0, 1 - self.place.core).wait_send()


class Share:
    def __init__(self, place, blocks, send_sem, recv_sem):
        self.place, self.blocks, self.send_sem, self.recv_sem = place, blocks, send_sem, recv_sem

    def hop(self, way, step, arriving):
        past = step + (1 if arriving else 0)
        source = (self.place.y + (2 * NY - past if way == 0 else past)) % NY
        n = self.blocks.shape[0]
        which = slice(0, n)
        if step == NY // 2 - 1:
            which = slice(way * (n // 2), (way + 1) * (n // 2))
        rows = self.blocks.at[which, span(source, BLK // NY)]
        device = self.place.over(1 if way == 0 else NY - 1)
        return send(rows, rows, self.send_sem.at[way, step], self.recv_sem.at[way, step], device)

    def advance(self, step):
        for way in range(2):
            if step:
                self.hop(way, step - 1, True).wait_recv()
            if step < NY // 2:
                self.hop(way, step, False).start()

    def leave(self):
        for way in range(2):
            for step in range(NY // 2):
                self.hop(way, step, False).wait_send()


class Move:
    def __init__(self, place, state, partner, held, own_sem, send_sem, recv_sem):
        self.place, self.partner, self.held = place, partner, held
        self.buffers = [state] + list(held)
        self.own_sem, self.send_sem, self.recv_sem = own_sem, send_sem, recv_sem

    def ends(self, stage):
        return self.buffers[(0, 1, 3, 4)[stage]], self.buffers[(1, 2, 4, 5)[stage]]

    def own(self, stage):
        src, dst = self.ends(stage)
        if stage % 2 == 0:
            here = self.place.z
            return pltpu.make_async_copy(src.at[here], dst.at[here], self.own_sem.at[stage])
        here = self.place.x * NCORE + self.place.core
        return pltpu.make_async_copy(src.at[:, here], dst.at[here], self.own_sem.at[stage])

    def piece(self, stage, k, core, arriving):
        place = self.place
        src, dst = self.ends(stage)
        if stage % 2 == 0:
            landing = (place.z + NZ - k) % NZ if arriving else place.z
            return send(
                src.at[(place.z + k) % NZ],
                dst.at[landing],
                self.send_sem.at[stage, k],
                self.recv_sem.at[stage, k],
                place.along(k),
            )
        other = (place.x + k) % NX * NCORE + core
        if arriving:
            return send(
                src.at[:, other],
                dst.at[other],
                self.send_sem.at[stage, k * NCORE + core],
                self.recv_sem.at[stage, k * NCORE + core],
                place.across(k, core),
            )
        return send(
            src.at[:, other],
            dst.at[place.x * NCORE + place.core],
            self.send_sem.at[stage, k * NCORE + core],
            self.recv_sem.at[stage, (NX - k) % NX * NCORE + place.core],
            place.across(k, core),
        )

    def pieces(self, stage, arriving):
        if stage % 2 == 0:
            return [self.piece(stage, k, 0, arriving) for k in range(1, NZ)]
        rest = [self.piece(stage, k, c, arriving) for k in range(1, NX) for c in range(NCORE)]
        return rest + [self.piece(stage, 0, 1 - self.place.core, arriving)]

    def start(self, stage):
        for copy in self.pieces(stage, False):
            copy.start()
        self.own(stage).start()

    def arrive(self, stage):
        for copy in self.pieces(stage, True):
            copy.wait_recv()
        self.own(stage).wait()

    def leave(self):
        for stage in range(4):
            for copy in self.pieces(stage, False):
                copy.wait_send()

    def order(self):
        def one(slot, carry):
            z, j = slot // PLANE, slot % PLANE
            expert = self.partner[j // NCORE * (NZ * NCORE) + z * NCORE + j % NCORE]
            j_from = expert // (NZ * NCORE) * NCORE + expert % NCORE
            self.held[2][z, j] = self.held[1][j_from, expert // NCORE % NZ]
            return carry

        lax.fori_loop(0, NZ * PLANE, one, 0)

    def tile(self, t):
        return self.held[4][t // 2 % PLANE, t // (2 * PLANE), span(t % 2, 16), :]


def dispatch_kernel(
    tok, og, meta, state, partner, xs, chosen, blocks, own_rows, moment, lay, ring, picked, choose, notes, relay,
    held_0, held_1, held_2, held_3, held_4,
    own_sem, notes_send, notes_recv, ring_send, ring_recv, out_own, out_send, out_recv, relay_send, relay_recv, keep_sem,
    move_own, move_send, move_recv, share_send, share_recv,
):
    count = tok.shape[0]
    chunks, _, width = ring.shape
    half = chunks // 2
    place = Place()
    z = place.z
    out = Exchange(place, picked, xs, relay, out_own, out_send, out_recv, relay_send, relay_recv)
    move = Move(place, state, partner, (held_0, held_1, held_2, held_3, held_4), move_own, move_send, move_recv)
    share = Share(place, blocks, share_send, share_recv)

    def own_copy(q):
        src = tok if q < half else og
        return pltpu.make_async_copy(
            src.at[:, (q % half) * width : (q % half + 1) * width],
            ring.at[q, span(z, count)],
            own_sem.at[q],
        )

    for q in range(chunks):
        own_copy(q).start()
    own_notes = pltpu.make_async_copy(meta.at[z], notes.at[z], keep_sem.at[1])
    own_notes.start()
    place.meet(True)

    def note(k, source):
        return send(
            meta.at[(z + k) % NZ], notes.at[source], notes_send.at[k], notes_recv.at[k], place.along(k)
        )

    for k in range(1, NZ):
        note(k, z).start()
    for q in range(chunks):
        own_copy(q).wait()
    own_notes.wait()
    move.start(0)

    def unpack():
        n = blocks.shape[0]

        def one(b, carry):
            rows = move.tile(b)
            own_rows[b] = rows
            blocks[b, span(place.y, BLK // NY), :] = rows
            moment[b] = move.tile(n + b).astype(jnp.float32) + move.tile(2 * n + b).astype(jnp.float32)
            return carry

        lax.fori_loop(0, n, one, 0)
        lay[...] = move.tile(3 * n)

    def hop(q, way, step, arriving):
        rows = count
        if way == 0:
            source = (z + 2 * NZ - step - (1 if arriving else 0)) % NZ
        else:
            source = (z + step + (1 if arriving else 0)) % NZ
        start = source * count
        if step == NZ // 2 - 1:
            rows = count // 2
            start = start + way * rows
        block = ring.at[q, pl.ds(pl.multiple_of(start, rows), rows)]
        return send(
            block,
            block,
            ring_send.at[q, way, step],
            ring_recv.at[q, way, step],
            place.along(1 if way == 0 else NZ - 1),
        )

    def keep():
        return pltpu.make_async_copy(choose.at[0], chosen, keep_sem.at[0])

    def build():
        for k in range(1, NZ):
            note(k, (z + NZ - k) % NZ).wait_recv()
        row = lax.broadcasted_iota(jnp.int32, (ROWS, count), 0).astype(jnp.float32)

        def fill(source, carry):
            both = notes[source].astype(jnp.float32)
            for other in range(PLANE):
                hit = row == both[other : other + 1, :]
                rows = slice(other * ROWS, (other + 1) * ROWS)
                scale = both[PLANE + other : PLANE + other + 1, :]
                choose[0, rows, span(source, count)] = jnp.where(hit, 1.0, 0.0).astype(jnp.bfloat16)
                choose[1, rows, span(source, count)] = jnp.where(hit, scale, 0.0).astype(jnp.bfloat16)
            return carry

        lax.fori_loop(0, NZ, fill, 0)
        keep().start()

    def step(i, carry):
        for s in range(NZ // 2):
            q = i - s

            @pl.when((q >= 0) & (q < chunks))
            def _():
                for way in range(2):
                    if s:
                        hop(q, way, s - 1, True).wait_recv()
                    hop(q, way, s, False).start()

        pl.when(i == 1)(build)

        @pl.when((i > NZ // 2) & (i <= NZ // 2 + chunks))
        def _():
            out.forward(i - NZ // 2 - 1)

        q = i - NZ // 2

        @pl.when((q >= 0) & (q < chunks))
        def _():
            for way in range(2):
                hop(q, way, NZ // 2 - 1, True).wait_recv()
            for h in (1, 0):
                rows = slice(h * (PLANE // 2) * ROWS, (h + 1) * (PLANE // 2) * ROWS)
                picked[q, rows, :] = dot(choose[q // half, rows, :], ring[q]).astype(jnp.bfloat16)
                out.start(q, (2, 3) if h else (1, 0))

        @pl.when(i == 1)
        def _():
            move.arrive(0)
            move.start(1)

        @pl.when(i == 2)
        def _():
            move.arrive(1)
            move.order()
            move.start(2)

        @pl.when(i == 4)
        def _():
            move.arrive(2)
            move.start(3)

        @pl.when(i == 5)
        def _():
            move.arrive(3)
            unpack()
            share.advance(0)

        for s in range(1, NY // 2 + 1):

            @pl.when(i == 5 + s)
            def _():
                share.advance(s)

        return carry

    lax.fori_loop(0, chunks + NZ // 2 + 1, step, 0)

    def finish(q, carry):
        for way in range(2):
            for s in range(NZ // 2):
                hop(q, way, s, False).wait_send()
        out.leave(q)
        out.arrive(q)
        return carry

    lax.fori_loop(0, chunks, finish, 0)
    for k in range(1, NZ):
        note(k, z).wait_send()
    keep().wait()
    move.leave()
    share.leave()


def dispatch(tokens, grads, meta, state, partner, tiles, chunks):
    count, features = tokens.shape
    width = 2 * features // chunks
    bf16 = jnp.bfloat16
    slots = PLANE * ROWS
    dma = pltpu.SemaphoreType.DMA
    anywhere = pl.BlockSpec(memory_space=pl.ANY)
    return pl.pallas_call(
        dispatch_kernel,
        in_specs=[anywhere] * 4 + [pl.BlockSpec(memory_space=pltpu.SMEM)],
        out_specs=[anywhere, anywhere] + [pl.BlockSpec(memory_space=pltpu.VMEM)] * 4,
        out_shape=[
            jax.ShapeDtypeStruct((chunks, slots, width), bf16),
            jax.ShapeDtypeStruct((slots, NZ * count), bf16),
            jax.ShapeDtypeStruct((tiles, BLK, BLK), bf16),
            jax.ShapeDtypeStruct((tiles, BLK // NY, BLK), bf16),
            jax.ShapeDtypeStruct((tiles, BLK // NY, BLK), jnp.float32),
            jax.ShapeDtypeStruct((BLK // NY, BLK), bf16),
        ],
        scratch_shapes=[
            pltpu.VMEM((chunks, NZ * count, width), bf16),
            pltpu.VMEM((chunks, slots, width), bf16),
            pltpu.VMEM((2, slots, NZ * count), bf16),
            pltpu.VMEM(meta.shape, bf16),
            pltpu.VMEM((chunks, 2, ROWS, width), bf16),
            *[pltpu.VMEM(state.shape, bf16)] * 5,
            dma((chunks,)),
            dma((NZ,)),
            dma((NZ,)),
            dma((chunks, 2, NZ // 2)),
            dma((chunks, 2, NZ // 2)),
            dma((chunks,)),
            dma((chunks, PLANE)),
            dma((chunks, PLANE)),
            dma((chunks, 2)),
            dma((chunks, 2)),
            dma((2,)),
            dma((4,)),
            dma((4, NZ)),
            dma((4, NZ)),
            dma((2, NY // 2)),
            dma((2, NY // 2)),
        ],
        compiler_params=pltpu.CompilerParams(
            collective_id=0, has_side_effects=True, vmem_limit_bytes=56 << 20
        ),
        cost_estimate=pl.CostEstimate(
            flops=2 * slots * NZ * count * 2 * features, bytes_accessed=300 << 20, transcendentals=0
        ),
    )(tokens, grads, meta, state, partner)


def return_kernel(
    pg, sc, choose, wg, own_blocks, old_moment, tg, score, moment, blocks,
    back, marks, relay, part, leaving, landed, sums, grads,
    x_own, x_send, x_recv, relay_send, relay_recv, mark_own, mark_send, mark_recv,
    z_send, z_recv, sum_send, sum_recv, y_send, y_recv, share_send, share_recv,
):
    chunks, slots, width = pg.shape
    count = tg.shape[0]
    last = NZ // 2 - 1
    place = Place()
    z, y = place.z, place.y
    cross = Exchange(place, pg, back, relay, x_own, x_send, x_recv, relay_send, relay_recv)
    mark = Exchange(place, sc, marks, None, mark_own, mark_send, mark_recv, None, None)

    own_grads = pltpu.make_async_copy(wg.at[y], grads.at[y], y_send.at[0])
    own_grads.start()
    place.meet(True)
    cross.start(0)

    def grad(k, landing):
        return send(wg.at[(y + k) % NY], grads.at[landing], y_send.at[k], y_recv.at[k], place.over(k))

    for k in range(1, NY):
        grad(k, y).start()
    mark.start(0)
    cross.start(1)
    cross.forward(0)

    share = Share(place, blocks, share_send, share_recv)

    def update():
        for k in range(1, NY):
            grad(k, (y + NY - k) % NY).wait_recv()
        own_grads.wait()

        def one(b, carry):
            total = DECAY * old_moment[b]
            for source in range(NY):
                total = total + grads[source, b].astype(jnp.float32)
            moment[b] = total
            fresh = own_blocks[b].astype(jnp.float32) - RATE * total
            blocks[b, span(y, BLK // NY), :] = fresh.astype(jnp.bfloat16)
            return carry

        lax.fori_loop(0, blocks.shape[0], one, 0)
        share.advance(0)

    def hop(q, way, step):
        rows = slice(0, count)
        if step == 0:
            rows = slice(way * (count // 2), (way + 1) * (count // 2))
        return send(
            leaving.at[q, way, step, rows],
            landed.at[q, way, step, rows],
            z_send.at[q, way, step],
            z_recv.at[q, way, step],
            place.along(1 if way == 0 else NZ - 1),
        )

    def target(way, step):
        if way == 0:
            return (z + NZ // 2 - step) % NZ
        return (z + NZ // 2 + step) % NZ

    def own_sum():
        return pltpu.make_async_copy(sums.at[z], score.at[z], sum_send.at[0])

    def summed(k, landing):
        return send(sums.at[(z + k) % NZ], score.at[landing], sum_send.at[k], sum_recv.at[k], place.along(k))

    def step(i, carry):
        @pl.when(i < chunks)
        def _():
            q = i
            cross.arrive(q)

            def add(t, carry):
                cols = span(t, 2 * count)
                part[q, cols, :] = dot(choose[:, cols], back[q], TN)
                return carry

            lax.fori_loop(0, NZ // 2, add, 0)
            for way in range(2):
                size = count // 2
                start = target(way, 0) * count + way * size
                rows = pl.ds(pl.multiple_of(start, size), size)
                leaving[q, way, 0, way * size : (way + 1) * size, :] = part[q, rows, :].astype(jnp.bfloat16)
                hop(q, way, 0).start()

        for s in range(1, NZ // 2):
            q = i - s

            @pl.when((q >= 0) & (q < chunks))
            def _():
                for way in range(2):
                    hop(q, way, s - 1).wait_recv()
                    mine = part[q, span(target(way, s), count), :]
                    if s == 1:
                        size = count // 2
                        near = slice(way * size, (way + 1) * size)
                        far = slice((1 - way) * size, (2 - way) * size)
                        more = landed[q, way, 0, near, :].astype(jnp.float32)
                        leaving[q, way, 1, near, :] = (mine[near] + more).astype(jnp.bfloat16)
                        leaving[q, way, 1, far, :] = mine[far].astype(jnp.bfloat16)
                    else:
                        more = landed[q, way, s - 1].astype(jnp.float32)
                        leaving[q, way, s] = (mine + more).astype(jnp.bfloat16)
                    hop(q, way, s).start()

        q = i - NZ // 2

        @pl.when(q >= 0)
        def _():
            total = part[q, span(z, count), :]
            for way in range(2):
                hop(q, way, last).wait_recv()
                total = total + landed[q, way, last].astype(jnp.float32)
            tg[:, pl.ds(pl.multiple_of(q * width, width), width)] = total.astype(jnp.bfloat16)

        @pl.when(i + 2 < chunks)
        def _():
            cross.start(i + 2)

        @pl.when(i + 1 < chunks)
        def _():
            cross.forward(i + 1)

        pl.when(i == 5)(update)
        for s in range(1, NY // 2 + 1):

            @pl.when(i == 5 + s)
            def _():
                share.advance(s)

        @pl.when(i == chunks - 1)
        def _():
            mark.arrive(0)
            spread = dot(marks[0], choose[...], TN)
            both = spread[:PLANE] + spread[PLANE : 2 * PLANE]
            for source in range(NZ):
                sums[source] = both[:, source * count : (source + 1) * count]
            own_sum().start()
            for k in range(1, NZ):
                summed(k, z).start()

        return carry

    lax.fori_loop(0, chunks + NZ // 2, step, 0)

    def finish(q, carry):
        cross.leave(q)
        for way in range(2):
            for s in range(NZ // 2):
                hop(q, way, s).wait_send()
        return carry

    lax.fori_loop(0, chunks, finish, 0)
    mark.leave(0)
    own_sum().wait()
    for k in range(1, NZ):
        summed(k, z).wait_send()
        summed(k, (z + NZ - k) % NZ).wait_recv()
    for k in range(1, NY):
        grad(k, y).wait_send()
    share.leave()


def give_back(pg, sc, choose, wg, own_blocks, old_moment, count):
    chunks, slots, width = pg.shape
    f32, bf16 = jnp.float32, jnp.bfloat16
    dma = pltpu.SemaphoreType.DMA
    anywhere = pl.BlockSpec(memory_space=pl.ANY)
    vmem = pl.BlockSpec(memory_space=pltpu.VMEM)
    return pl.pallas_call(
        return_kernel,
        in_specs=[anywhere, anywhere, vmem, anywhere, vmem, vmem],
        out_specs=[vmem, anywhere, vmem, vmem],
        out_shape=[
            jax.ShapeDtypeStruct((count, chunks * width), bf16),
            jax.ShapeDtypeStruct((NZ, PLANE, count), f32),
            jax.ShapeDtypeStruct(old_moment.shape, f32),
            jax.ShapeDtypeStruct((wg.shape[1], BLK, BLK), bf16),
        ],
        scratch_shapes=[
            pltpu.VMEM((chunks, slots, width), bf16),
            pltpu.VMEM(sc.shape, bf16),
            pltpu.VMEM((chunks, 2, ROWS, width), bf16),
            pltpu.VMEM((chunks, NZ * count, width), f32),
            pltpu.VMEM((chunks, 2, NZ // 2, count, width), bf16),
            pltpu.VMEM((chunks, 2, NZ // 2, count, width), bf16),
            pltpu.VMEM((NZ, PLANE, count), f32),
            pltpu.VMEM(wg.shape, bf16),
            dma((chunks,)),
            dma((chunks, PLANE)),
            dma((chunks, PLANE)),
            dma((chunks, 2)),
            dma((chunks, 2)),
            dma((1,)),
            dma((1, PLANE)),
            dma((1, PLANE)),
            dma((chunks, 2, NZ // 2)),
            dma((chunks, 2, NZ // 2)),
            dma((NZ,)),
            dma((NZ,)),
            dma((NY,)),
            dma((NY,)),
            dma((2, NY // 2)),
            dma((2, NY // 2)),
        ],
        compiler_params=pltpu.CompilerParams(
            collective_id=1, has_side_effects=True, vmem_limit_bytes=56 << 20
        ),
        cost_estimate=pl.CostEstimate(
            flops=2 * slots * NZ * count * chunks * width, bytes_accessed=150 << 20, transcendentals=0
        ),
    )(pg, sc, choose, wg, own_blocks, old_moment)


def pack_state(own_blocks, moments, layout_one):
    bf16 = jnp.bfloat16
    high = moments.astype(bf16)
    low = (moments - high.astype(jnp.float32)).astype(bf16)
    flat_layout = layout_one.reshape(-1)
    lay_tile = jnp.pad(flat_layout, (0, 16 * BLK - flat_layout.size)).astype(bf16)
    parts = [a.reshape(-1, 16, BLK) for a in (own_blocks, high, low, lay_tile)]
    count = sum(a.shape[0] for a in parts)
    parts.append(jnp.zeros((2 * NZ * PLANE - count, 16, BLK), bf16))
    return jnp.concatenate(parts).reshape(NZ, PLANE, 32, BLK)


def body(tokens, out_grad, expert_ids, route_weights, blocks, layout, moments, partner):
    f32, bf16 = jnp.float32, jnp.bfloat16
    n = lax.axis_size("expert")
    n_dp = lax.axis_size("dp")
    count, width = tokens.shape
    share = BLK // n_dp
    own = lax.dynamic_slice_in_dim(blocks[0], lax.axis_index("dp") * share, share, 2)
    state = pack_state(own, moments[0], layout[0])
    tiles = own.shape[0] * own.shape[1]

    place = Place()
    number = jnp.arange(n, dtype=jnp.int32)
    where = (place.x + number // NCORE % NX) % NX * (NZ * NCORE) + number // PLANE * NCORE + number % NCORE
    holds = partner[where]
    picks = expert_ids[None] == holds[:, None, None]
    named = jnp.any(picks, axis=2)
    before = jnp.tril(jnp.ones((count, count), bf16), -1)
    rank = dot(named.astype(bf16), before, NT)
    weight = jnp.sum(jnp.where(picks, route_weights[None].astype(f32), 0.0), axis=2)
    slot = jnp.where(named, rank + (place.z * CAP).astype(f32), -1.0)
    meta = jnp.concatenate(
        [slot.reshape(NZ, PLANE, count), weight.reshape(NZ, PLANE, count)], axis=1
    ).astype(bf16)
    xs, choose, mats, own, old_moment, lay = dispatch(
        tokens, out_grad, meta, state, partner, tiles, 8
    )
    layout_one = lay.reshape(-1)[: layout[0].size].astype(jnp.int32).reshape(layout[0].shape)
    pg, sc, wg = expert_compute(
        layout_one, place.core.reshape(1), xs, mats.reshape(blocks[0].shape), 448
    )
    token_grad, score, moment, updated = give_back(
        pg, sc[None], choose, wg, own, old_moment, count
    )
    score = jnp.sum(jnp.where(picks, score.reshape(n, count)[:, :, None], 0.0), axis=0)
    route_grad = (score / route_weights.astype(f32)).astype(bf16)
    return (
        token_grad,
        route_grad,
        updated.reshape(blocks.shape),
        moment.reshape(moments.shape),
    )


def solution(mesh):
    rows = P(("dp", "expert"), None)
    state = P("expert", None, None, None, None)
    moment = P("expert", None, None, "dp", None)
    return jax.shard_map(
        body,
        mesh=mesh,
        in_specs=(rows, rows, rows, rows, state, P("expert", None, None, None), moment, P()),
        out_specs=(rows, rows, state, moment),
        check_vma=False,
    )
```

```python
import functools

import jax
import jax.numpy as jnp
from jax import lax
from jax.experimental import pallas as pl
from jax.experimental.pallas import tpu as pltpu
from jax.sharding import PartitionSpec as P

HID = 1408
BLK = 128
CAP = 14
DECAY = 0.9
RATE = 0.01

NT = (((1,), (1,)), ((), ()))
TN = (((0,), (0,)), ((), ()))


def dot(a, b, dims=(((1,), (0,)), ((), ()))):
    return lax.dot_general(a, b, dims, preferred_element_type=jnp.float32)


def lanes(i):
    return pl.ds(pl.multiple_of(i * BLK, BLK), BLK)


def expert_kernel(lay, place_ref, x_ref, s_ref, w_ref, pg_ref, sc_ref, out_ref, wg_ref, gate, up, hg, hid, gg, ug, acc):
    nb = w_ref.shape[1]
    rows = x_ref.shape[1]
    per = x_ref.shape[2] // BLK

    def chunk(ref, i):
        return ref[i // per, :, lanes(i % per)]

    @pl.when(pl.program_id(0) == 0)
    def _():
        wg_ref[...] = jnp.zeros_like(wg_ref)

    gate[...] = jnp.zeros_like(gate)
    up[...] = jnp.zeros_like(up)
    hg[...] = jnp.zeros_like(hg)

    def first(b, carry):
        gate[:, lanes(lay[0, b, 1])] += dot(chunk(x_ref, lay[0, b, 0]), w_ref[0, b])
        up[:, lanes(lay[1, b, 1])] += dot(chunk(x_ref, lay[1, b, 0]), w_ref[1, b])
        hg[:, lanes(lay[2, b, 0])] += dot(chunk(s_ref, lay[2, b, 1]), w_ref[2, b], NT)
        return carry

    lax.fori_loop(0, nb, first, 0)

    def middle(j, score):
        g = gate[:, lanes(j)]
        u = up[:, lanes(j)]
        h = hg[:, lanes(j)]
        sig = jax.nn.sigmoid(g)
        act = g * sig
        hb = (act * u).astype(jnp.bfloat16)
        hid[:, lanes(j)] = hb
        gg[:, lanes(j)] = (h * u * sig * (1.0 + g * (1.0 - sig))).astype(jnp.bfloat16)
        ug[:, lanes(j)] = (h * act).astype(jnp.bfloat16)
        return score + hb.astype(jnp.float32) * h

    score = lax.fori_loop(0, HID // BLK, middle, jnp.zeros((rows, BLK), jnp.float32))
    total = jnp.sum(score, axis=1, keepdims=True)
    high = total.astype(jnp.bfloat16).astype(jnp.float32)
    lane = lax.broadcasted_iota(jnp.int32, (rows, BLK), 1)
    group = pl.program_id(0) * (rows // (NCORE * ROWS))
    for k in range(1, rows // (NCORE * ROWS)):
        group = group + (lax.broadcasted_iota(jnp.int32, (rows, BLK), 0) >= k * NCORE * ROWS).astype(jnp.int32)
    place = jnp.where(group == 0, 0, NX - group) * NCORE + place_ref[0]
    sc_ref[...] = jnp.where(
        lane == place, high, jnp.where(lane == place + 8, total - high, 0.0)
    ).astype(jnp.bfloat16)

    acc[...] = jnp.zeros_like(acc)

    def last(b, carry):
        r0, c0, r1, c1 = lay[0, b, 0], lay[0, b, 1], lay[1, b, 0], lay[1, b, 1]
        acc[:, lanes(r0)] += dot(gg[:, lanes(c0)], w_ref[0, b], NT)
        acc[:, lanes(r1)] += dot(ug[:, lanes(c1)], w_ref[1, b], NT)
        wg_ref[0, b] += dot(chunk(x_ref, r0), gg[:, lanes(c0)], TN)
        wg_ref[1, b] += dot(chunk(x_ref, r1), ug[:, lanes(c1)], TN)
        wg_ref[2, b] += dot(hid[:, lanes(lay[2, b, 0])], chunk(s_ref, lay[2, b, 1]), TN)
        return carry

    lax.fori_loop(0, nb, last, 0)
    for q in range(pg_ref.shape[0]):
        width = pg_ref.shape[2]
        pg_ref[q] = acc[:, q * width : (q + 1) * width].astype(jnp.bfloat16)

    @pl.when(pl.program_id(0) == pl.num_programs(0) - 1)
    def _():
        share = out_ref.shape[2]
        for y in range(out_ref.shape[0]):
            for m in range(w_ref.shape[0]):
                out_ref[y, m * nb : (m + 1) * nb] = wg_ref[m, :, y * share : (y + 1) * share, :].astype(jnp.bfloat16)


def expert_compute(layout_one, place, xs, mats, tile):
    nq, rows, width = xs.shape
    nq = nq // 2
    nm, nb = mats.shape[:2]
    row_spec = pl.BlockSpec((nq, tile, width), lambda i, lay, place: (0, i, 0))
    grad_spec = pl.BlockSpec((nq, tile, width), lambda i, lay, place: (1, i, 0))
    f32, bf16 = jnp.float32, jnp.bfloat16
    return pl.pallas_call(
        expert_kernel,
        grid_spec=pltpu.PrefetchScalarGridSpec(
            num_scalar_prefetch=2,
            grid=(rows // tile,),
            in_specs=[
                row_spec,
                grad_spec,
                pl.BlockSpec((nm, nb, BLK, BLK), lambda i, lay, place: (0, 0, 0, 0)),
            ],
            out_specs=[
                pl.BlockSpec((2 * nq, tile, width // 2), lambda i, lay, place: (0, i, 0)),
                pl.BlockSpec((tile, BLK), lambda i, lay, place: (i, 0)),
                pl.BlockSpec((NY, nm * nb, BLK // NY, BLK), lambda i, lay, place: (0, 0, 0, 0)),
            ],
            scratch_shapes=[
                pltpu.VMEM(mats.shape, f32),
                pltpu.VMEM((tile, HID), f32),
                pltpu.VMEM((tile, HID), f32),
                pltpu.VMEM((tile, HID), f32),
                pltpu.VMEM((tile, HID), bf16),
                pltpu.VMEM((tile, HID), bf16),
                pltpu.VMEM((tile, HID), bf16),
                pltpu.VMEM((tile, nq * width), f32),
            ],
        ),
        out_shape=[
            jax.ShapeDtypeStruct((2 * nq, rows, width // 2), bf16),
            jax.ShapeDtypeStruct((rows, BLK), bf16),
            jax.ShapeDtypeStruct((NY, nm * nb, BLK // NY, BLK), bf16),
        ],
        compiler_params=pltpu.CompilerParams(vmem_limit_bytes=56 << 20),
        cost_estimate=pl.CostEstimate(
            flops=8 * nb * rows * BLK * BLK * 2,
            bytes_accessed=3 * xs.size + mats.size * 6,
            transcendentals=rows * HID,
        ),
    )(layout_one, place, xs, xs, mats)


NX, NZ, NCORE, NY = 4, 8, 2, 8
PLANE = NX * NCORE
ROWS = NZ * CAP
MESH = pl.DeviceIdType.MESH


class Place:
    def __init__(self):
        me = lax.axis_index("expert")
        self.y = lax.axis_index("dp")
        self.me = me
        self.x = me // (NZ * NCORE)
        self.z = (me // NCORE) % NZ
        self.core = me % NCORE

    def along(self, dz):
        return (self.y, self.x * (NZ * NCORE) + (self.z + dz) % NZ * NCORE + self.core)

    def across(self, dx, core):
        return (self.y, (self.x + dx) % NX * (NZ * NCORE) + self.z * NCORE + core)

    def over(self, dy):
        return ((self.y + dy) % NY, self.me)

    def meet(self, with_y):
        others = [self.along(k) for k in range(1, NZ)]
        others += [self.across(dx, c) for dx in range(1, NX) for c in range(NCORE)]
        others.append(self.across(0, 1 - self.core))
        if with_y:
            others += [self.over(k) for k in range(1, NY)]
        barrier = pltpu.get_barrier_semaphore()
        for other in others:
            pl.semaphore_signal(barrier, inc=1, device_id=other, device_id_type=MESH)
        pl.semaphore_wait(barrier, len(others))


def send(src, dst, send_sem, recv_sem, device):
    return pltpu.make_async_remote_copy(
        src_ref=src,
        dst_ref=dst,
        send_sem=send_sem,
        recv_sem=recv_sem,
        device_id=device,
        device_id_type=MESH,
    )


def span(i, size):
    return pl.ds(pl.multiple_of(i * size, size), size)


class Exchange:
    far = NX // 2

    def __init__(self, place, src, dst, relay, own_sem, send_sem, recv_sem, relay_send, relay_recv):
        self.place, self.src, self.dst, self.relay = place, src, dst, relay
        self.own_sem, self.send_sem, self.recv_sem = own_sem, send_sem, recv_sem
        self.relay_send, self.relay_recv = relay_send, relay_recv

    def direct(self, q, dx, core):
        number = dx * NCORE + core
        landing = (NX - dx) % NX * NCORE + self.place.core
        return send(
            self.src.at[q, span(number, ROWS)],
            self.dst.at[q, span(landing, ROWS)],
            self.send_sem.at[q, number],
            self.recv_sem.at[q, landing],
            self.place.across(dx, core),
        )

    def first_leg(self, q, way):
        number = self.far * NCORE + way
        return send(
            self.src.at[q, span(number, ROWS)],
            self.relay.at[q, way],
            self.send_sem.at[q, number],
            self.relay_recv.at[q, way],
            self.place.across(1 if way == 0 else NX - 1, self.place.core),
        )

    def second_leg(self, q, way):
        landing = self.far * NCORE + self.place.core
        return send(
            self.relay.at[q, way],
            self.dst.at[q, span(landing, ROWS)],
            self.relay_send.at[q, way],
            self.recv_sem.at[q, landing],
            self.place.across(1 if way == 0 else NX - 1, way),
        )

    def own(self, q):
        rows = span(self.place.core, ROWS)
        return pltpu.make_async_copy(self.src.at[q, rows], self.dst.at[q, rows], self.own_sem.at[q])

    def start(self, q, steps=(2, 1, 3, 0)):
        for dx in steps:
            if dx == 0:
                self.direct(q, 0, 1 - self.place.core).start()
                self.own(q).start()
            elif dx == self.far and self.relay is not None:
                for way in range(2):
                    self.first_leg(q, way).start()
            else:
                for core in range(NCORE):
                    self.direct(q, dx, core).start()

    def forward(self, q):
        for way in range(2):
            self.first_leg(q, way).wait_recv()
            self.second_leg(q, way).start()

    def arrive(self, q):
        def one(landing):
            part = self.dst.at[q, span(landing, ROWS)]
            send(part, part, self.send_sem.at[q, landing], self.recv_sem.at[q, landing], self.place.across(1, 0)).wait_recv()

        for dx in range(1, NX):
            for core in range(NCORE):
                one(dx * NCORE + core)
        one(1 - self.place.core)
        self.own(q).wait()

    def leave(self, q):
        for dx in range(1, NX):
            for core in range(NCORE):
                if dx == self.far and self.relay is not None:
                    self.first_leg(q, core).wait_send()
                    self.second_leg(q, core).wait_send()
                else:
                    self.direct(q, dx, core).wait_send()
        self.direct(q, 0, 1 - self.place.core).wait_send()


class Share:
    def __init__(self, place, blocks, send_sem, recv_sem):
        self.place, self.blocks, self.send_sem, self.recv_sem = place, blocks, send_sem, recv_sem

    def hop(self, way, step, arriving):
        past = step + (1 if arriving else 0)
        source = (self.place.y + (2 * NY - past if way == 0 else past)) % NY
        n = self.blocks.shape[0]
        which = slice(0, n)
        if step == NY // 2 - 1:
            which = slice(way * (n // 2), (way + 1) * (n // 2))
        rows = self.blocks.at[which, span(source, BLK // NY)]
        device = self.place.over(1 if way == 0 else NY - 1)
        return send(rows, rows, self.send_sem.at[way, step], self.recv_sem.at[way, step], device)

    def advance(self, step):
        for way in range(2):
            if step:
                self.hop(way, step - 1, True).wait_recv()
            if step < NY // 2:
                self.hop(way, step, False).start()

    def leave(self):
        for way in range(2):
            for step in range(NY // 2):
                self.hop(way, step, False).wait_send()


class Move:
    def __init__(self, place, state, partner, held, own_sem, send_sem, recv_sem):
        self.place, self.partner, self.held = place, partner, held
        self.buffers = [state] + list(held)
        self.own_sem, self.send_sem, self.recv_sem = own_sem, send_sem, recv_sem

    def ends(self, stage):
        return self.buffers[(0, 1, 3, 4)[stage]], self.buffers[(1, 2, 4, 5)[stage]]

    def own(self, stage):
        src, dst = self.ends(stage)
        if stage % 2 == 0:
            here = self.place.z
            return pltpu.make_async_copy(src.at[here], dst.at[here], self.own_sem.at[stage])
        here = self.place.x * NCORE + self.place.core
        return pltpu.make_async_copy(src.at[:, here], dst.at[here], self.own_sem.at[stage])

    def piece(self, stage, k, core, arriving):
        place = self.place
        src, dst = self.ends(stage)
        if stage % 2 == 0:
            landing = (place.z + NZ - k) % NZ if arriving else place.z
            return send(
                src.at[(place.z + k) % NZ],
                dst.at[landing],
                self.send_sem.at[stage, k],
                self.recv_sem.at[stage, k],
                place.along(k),
            )
        other = (place.x + k) % NX * NCORE + core
        if arriving:
            return send(
                src.at[:, other],
                dst.at[other],
                self.send_sem.at[stage, k * NCORE + core],
                self.recv_sem.at[stage, k * NCORE + core],
                place.across(k, core),
            )
        return send(
            src.at[:, other],
            dst.at[place.x * NCORE + place.core],
            self.send_sem.at[stage, k * NCORE + core],
            self.recv_sem.at[stage, (NX - k) % NX * NCORE + place.core],
            place.across(k, core),
        )

    def pieces(self, stage, arriving):
        if stage % 2 == 0:
            return [self.piece(stage, k, 0, arriving) for k in range(1, NZ)]
        rest = [self.piece(stage, k, c, arriving) for k in range(1, NX) for c in range(NCORE)]
        return rest + [self.piece(stage, 0, 1 - self.place.core, arriving)]

    def start(self, stage):
        for copy in self.pieces(stage, False):
            copy.start()
        self.own(stage).start()

    def arrive(self, stage):
        for copy in self.pieces(stage, True):
            copy.wait_recv()
        self.own(stage).wait()

    def leave(self):
        for stage in range(4):
            for copy in self.pieces(stage, False):
                copy.wait_send()

    def order(self):
        def one(slot, carry):
            z, j = slot // PLANE, slot % PLANE
            expert = self.partner[j // NCORE * (NZ * NCORE) + z * NCORE + j % NCORE]
            j_from = expert // (NZ * NCORE) * NCORE + expert % NCORE
            self.held[2][z, j] = self.held[1][j_from, expert // NCORE % NZ]
            return carry

        lax.fori_loop(0, NZ * PLANE, one, 0)

    def tile(self, t):
        return self.held[4][t % PLANE, t // PLANE]


def dispatch_kernel(
    tok, og, meta, state, late_state, partner, xs, chosen, blocks, own_rows, moment, lay, ring, picked, choose, turned, notes, relay,
    held_0, held_1, held_2, held_3, held_4, late_0, late_1, late_2, late_3, late_4,
    own_sem, notes_send, notes_recv, ring_send, ring_recv, out_own, out_send, out_recv, relay_send, relay_recv, keep_sem,
    move_own, move_send, move_recv, share_send, share_recv, late_own, late_send, late_recv,
):
    count = tok.shape[0]
    chunks, _, width = ring.shape
    half = chunks // 2
    place = Place()
    z = place.z
    out = Exchange(place, picked, xs, relay, out_own, out_send, out_recv, relay_send, relay_recv)
    move = Move(place, state, partner, (held_0, held_1, held_2, held_3, held_4), move_own, move_send, move_recv)
    late = Move(place, late_state, partner, (late_0, late_1, late_2, late_3, late_4), late_own, late_send, late_recv)
    share = Share(place, blocks, share_send, share_recv)

    def own_copy(q):
        src = tok if q < half else og
        return pltpu.make_async_copy(
            src.at[:, (q % half) * width : (q % half + 1) * width],
            ring.at[q, span(z, count)],
            own_sem.at[q],
        )

    for q in range(chunks):
        own_copy(q).start()
    own_notes = pltpu.make_async_copy(meta.at[z], notes.at[z], keep_sem.at[1])
    own_notes.start()
    place.meet(True)

    def note(k, source):
        return send(
            meta.at[(z + k) % NZ], notes.at[source], notes_send.at[k], notes_recv.at[k], place.along(k)
        )

    for k in range(1, NZ):
        note(k, z).start()
    for q in range(chunks):
        own_copy(q).wait()
    own_notes.wait()
    move.start(0)

    def unpack():
        n = blocks.shape[0]

        def one(b, carry):
            rows = move.tile(b)
            own_rows[b] = rows
            blocks[b, span(place.y, BLK // NY), :] = rows
            return carry

        lax.fori_loop(0, n, one, 0)
        lay[...] = move.tile(n)

    def unpack_late():
        def one(b, carry):
            moment[b] = late.tile(b)
            return carry

        lax.fori_loop(0, moment.shape[0], one, 0)

    def hop(q, way, step, arriving):
        rows = count
        if way == 0:
            source = (z + 2 * NZ - step - (1 if arriving else 0)) % NZ
        else:
            source = (z + step + (1 if arriving else 0)) % NZ
        start = source * count
        if step == NZ // 2 - 1:
            rows = count // 2
            start = start + way * rows
        block = ring.at[q, pl.ds(pl.multiple_of(start, rows), rows)]
        return send(
            block,
            block,
            ring_send.at[q, way, step],
            ring_recv.at[q, way, step],
            place.along(1 if way == 0 else NZ - 1),
        )

    def keep():
        return pltpu.make_async_copy(turned, chosen, keep_sem.at[0])

    def build():
        for k in range(1, NZ):
            note(k, (z + NZ - k) % NZ).wait_recv()
        row = lax.broadcasted_iota(jnp.int32, (ROWS, count), 0).astype(jnp.float32)

        def fill(source, carry):
            both = notes[source].astype(jnp.float32)
            for other in range(PLANE):
                hit = row == both[other : other + 1, :]
                rows = slice(other * ROWS, (other + 1) * ROWS)
                scale = both[PLANE + other : PLANE + other + 1, :]
                choose[0, rows, span(source, count)] = jnp.where(hit, 1.0, 0.0).astype(jnp.bfloat16)
                choose[1, rows, span(source, count)] = jnp.where(hit, scale, 0.0).astype(jnp.bfloat16)
            return carry

        lax.fori_loop(0, NZ, fill, 0)

    def turn():
        def one(source, carry):
            block = choose[0, :, span(source, count)].astype(jnp.float32)
            turned[span(source, count), :] = block.T.astype(jnp.bfloat16)
            return carry

        lax.fori_loop(0, NZ, one, 0)
        keep().start()

    def step(i, carry):
        for s in range(NZ // 2):
            q = i - s

            @pl.when((q >= 0) & (q < chunks))
            def _():
                for way in range(2):
                    if s:
                        hop(q, way, s - 1, True).wait_recv()
                    hop(q, way, s, False).start()

        pl.when(i == 1)(build)
        pl.when(i == NZ // 2 + 3)(turn)

        q = i - NZ // 2

        @pl.when((q >= 0) & (q < chunks))
        def _():
            for way in range(2):
                hop(q, way, NZ // 2 - 1, True).wait_recv()
            for h in (1, 0):
                rows = slice(h * (PLANE // 2) * ROWS, (h + 1) * (PLANE // 2) * ROWS)
                picked[q, rows, :] = dot(choose[q // half, rows, :], ring[q]).astype(jnp.bfloat16)
                out.start(q, (2, 3) if h else (1, 0))

        @pl.when((i > NZ // 2) & (i <= NZ // 2 + chunks))
        def _():
            out.forward(i - NZ // 2 - 1)

        @pl.when(i == 1)
        def _():
            move.arrive(0)
            move.start(1)

        @pl.when(i == 2)
        def _():
            move.arrive(1)
            move.order()
            move.start(2)

        @pl.when(i == 4)
        def _():
            move.arrive(2)
            move.start(3)

        @pl.when(i == 5)
        def _():
            move.arrive(3)
            unpack()
            share.advance(0)

        for s in range(1, NY // 2 + 1):

            @pl.when(i == 5 + s)
            def _():
                share.advance(s)

        @pl.when(i == chunks)
        def _():
            late.start(0)

        @pl.when(i == chunks + 1)
        def _():
            late.arrive(0)
            late.start(1)

        @pl.when(i == chunks + 2)
        def _():
            late.arrive(1)
            late.order()
            late.start(2)

        @pl.when(i == chunks + 3)
        def _():
            late.arrive(2)
            late.start(3)

        @pl.when(i == chunks + 4)
        def _():
            late.arrive(3)
            unpack_late()

        return carry

    lax.fori_loop(0, chunks + NZ // 2 + 1, step, 0)

    def finish(q, carry):
        for way in range(2):
            for s in range(NZ // 2):
                hop(q, way, s, False).wait_send()
        out.leave(q)
        out.arrive(q)
        return carry

    lax.fori_loop(0, chunks, finish, 0)
    for k in range(1, NZ):
        note(k, z).wait_send()
    keep().wait()
    move.leave()
    late.leave()
    share.leave()


def dispatch(tokens, grads, meta, state, late_state, partner, tiles, chunks):
    count, features = tokens.shape
    width = 2 * features // chunks
    bf16 = jnp.bfloat16
    slots = PLANE * ROWS
    dma = pltpu.SemaphoreType.DMA
    anywhere = pl.BlockSpec(memory_space=pl.ANY)
    return pl.pallas_call(
        dispatch_kernel,
        in_specs=[anywhere] * 5 + [pl.BlockSpec(memory_space=pltpu.SMEM)],
        out_specs=[anywhere, anywhere] + [pl.BlockSpec(memory_space=pltpu.VMEM)] * 4,
        out_shape=[
            jax.ShapeDtypeStruct((chunks, slots, width), bf16),
            jax.ShapeDtypeStruct((NZ * count, slots), bf16),
            jax.ShapeDtypeStruct((tiles, BLK, BLK), bf16),
            jax.ShapeDtypeStruct((tiles, BLK // NY, BLK), bf16),
            jax.ShapeDtypeStruct((tiles, BLK // NY, BLK), bf16),
            jax.ShapeDtypeStruct((BLK // NY, BLK), bf16),
        ],
        scratch_shapes=[
            pltpu.VMEM((chunks, NZ * count, width), bf16),
            pltpu.VMEM((chunks, slots, width), bf16),
            pltpu.VMEM((2, slots, NZ * count), bf16),
            pltpu.VMEM((NZ * count, slots), bf16),
            pltpu.VMEM(meta.shape, bf16),
            pltpu.VMEM((chunks, 2, ROWS, width), bf16),
            *[pltpu.VMEM(state.shape, bf16)] * 10,
            dma((chunks,)),
            dma((NZ,)),
            dma((NZ,)),
            dma((chunks, 2, NZ // 2)),
            dma((chunks, 2, NZ // 2)),
            dma((chunks,)),
            dma((chunks, PLANE)),
            dma((chunks, PLANE)),
            dma((chunks, 2)),
            dma((chunks, 2)),
            dma((2,)),
            dma((4,)),
            dma((4, NZ)),
            dma((4, NZ)),
            dma((2, NY // 2)),
            dma((2, NY // 2)),
            dma((4,)),
            dma((4, NZ)),
            dma((4, NZ)),
        ],
        compiler_params=pltpu.CompilerParams(
            collective_id=0, has_side_effects=True, vmem_limit_bytes=56 << 20
        ),
        cost_estimate=pl.CostEstimate(
            flops=2 * slots * NZ * count * 2 * features, bytes_accessed=300 << 20, transcendentals=0
        ),
    )(tokens, grads, meta, state, late_state, partner)


def return_kernel(
    pg, sc, choose, wg, own_blocks, old_moment, tg, score, moment, blocks,
    back, marks, relay, part, leaving, landed, sums, grads,
    x_own, x_send, x_recv, relay_send, relay_recv, mark_own, mark_send, mark_recv,
    z_send, z_recv, sum_send, sum_recv, y_send, y_recv, share_send, share_recv,
):
    chunks, slots, width = pg.shape
    count = tg.shape[0]
    last = NZ // 2 - 1
    place = Place()
    z, y = place.z, place.y
    cross = Exchange(place, pg, back, relay, x_own, x_send, x_recv, relay_send, relay_recv)
    mark = Exchange(place, sc, marks, None, mark_own, mark_send, mark_recv, None, None)

    own_grads = pltpu.make_async_copy(wg.at[y], grads.at[y], y_send.at[0])
    own_grads.start()
    place.meet(True)
    cross.start(0)

    def grad(k, landing):
        return send(wg.at[(y + k) % NY], grads.at[landing], y_send.at[k], y_recv.at[k], place.over(k))

    for k in range(1, NY):
        grad(k, y).start()
    cross.start(1)
    cross.forward(0)
    cross.start(2)
    mark.start(0)
    cross.forward(1)

    share = Share(place, blocks, share_send, share_recv)

    def update():
        for k in range(1, NY):
            grad(k, (y + NY - k) % NY).wait_recv()
        own_grads.wait()

        def one(b, carry):
            total = DECAY * old_moment[b].astype(jnp.float32)
            for source in range(NY):
                total = total + grads[source, b].astype(jnp.float32)
            moment[b] = total
            fresh = own_blocks[b].astype(jnp.float32) - RATE * total
            blocks[b, span(y, BLK // NY), :] = fresh.astype(jnp.bfloat16)
            return carry

        lax.fori_loop(0, blocks.shape[0], one, 0)
        share.advance(0)

    def hop(q, way, step):
        rows = slice(0, count)
        if step == 0:
            rows = slice(way * (count // 2), (way + 1) * (count // 2))
        return send(
            leaving.at[q, way, step, rows],
            landed.at[q, way, step, rows],
            z_send.at[q, way, step],
            z_recv.at[q, way, step],
            place.along(1 if way == 0 else NZ - 1),
        )

    def target(way, step):
        if way == 0:
            return (z + NZ // 2 - step) % NZ
        return (z + NZ // 2 + step) % NZ

    def own_sum():
        return pltpu.make_async_copy(sums.at[z], score.at[z], sum_send.at[0])

    def summed(k, landing):
        return send(sums.at[(z + k) % NZ], score.at[landing], sum_send.at[k], sum_recv.at[k], place.along(k))

    def step(i, carry):
        @pl.when(i < chunks)
        def _():
            q = i
            cross.arrive(q)

            def add(t, carry):
                cols = span(t, 2 * count)
                part[q, cols, :] = dot(choose[cols, :], back[q])
                return carry

            lax.fori_loop(0, NZ // 2, add, 0)
            for way in range(2):
                size = count // 2
                start = target(way, 0) * count + way * size
                rows = pl.ds(pl.multiple_of(start, size), size)
                leaving[q, way, 0, way * size : (way + 1) * size, :] = part[q, rows, :].astype(jnp.bfloat16)
                hop(q, way, 0).start()

        for s in range(1, NZ // 2):
            q = i - s

            @pl.when((q >= 0) & (q < chunks))
            def _():
                for way in range(2):
                    hop(q, way, s - 1).wait_recv()
                    mine = part[q, span(target(way, s), count), :]
                    if s == 1:
                        size = count // 2
                        near = slice(way * size, (way + 1) * size)
                        far = slice((1 - way) * size, (2 - way) * size)
                        more = landed[q, way, 0, near, :].astype(jnp.float32)
                        leaving[q, way, 1, near, :] = (mine[near] + more).astype(jnp.bfloat16)
                        leaving[q, way, 1, far, :] = mine[far].astype(jnp.bfloat16)
                    else:
                        more = landed[q, way, s - 1].astype(jnp.float32)
                        leaving[q, way, s] = (mine + more).astype(jnp.bfloat16)
                    hop(q, way, s).start()

        q = i - NZ // 2

        @pl.when(q >= 0)
        def _():
            total = part[q, span(z, count), :]
            for way in range(2):
                hop(q, way, last).wait_recv()
                total = total + landed[q, way, last].astype(jnp.float32)
            tg[:, pl.ds(pl.multiple_of(q * width, width), width)] = total.astype(jnp.bfloat16)

        @pl.when(i + 3 < chunks)
        def _():
            cross.start(i + 3)

        @pl.when(i + 2 < chunks)
        def _():
            cross.forward(i + 2)

        pl.when(i == 5)(update)
        for s in range(1, NY // 2 + 1):

            @pl.when(i == 5 + s)
            def _():
                share.advance(s)

        @pl.when(i == chunks - 1)
        def _():
            mark.arrive(0)
            spread = dot(marks[0], choose[...], (((0,), (1,)), ((), ())))
            both = spread[:PLANE] + spread[PLANE : 2 * PLANE]
            for source in range(NZ):
                sums[source] = both[:, source * count : (source + 1) * count]
            own_sum().start()
            for k in range(1, NZ):
                summed(k, z).start()

        return carry

    lax.fori_loop(0, chunks + NZ // 2, step, 0)

    def finish(q, carry):
        cross.leave(q)
        for way in range(2):
            for s in range(NZ // 2):
                hop(q, way, s).wait_send()
        return carry

    lax.fori_loop(0, chunks, finish, 0)
    mark.leave(0)
    own_sum().wait()
    for k in range(1, NZ):
        summed(k, z).wait_send()
        summed(k, (z + NZ - k) % NZ).wait_recv()
    for k in range(1, NY):
        grad(k, y).wait_send()
    share.leave()


def give_back(pg, sc, choose, wg, own_blocks, old_moment, count):
    chunks, slots, width = pg.shape
    f32, bf16 = jnp.float32, jnp.bfloat16
    dma = pltpu.SemaphoreType.DMA
    anywhere = pl.BlockSpec(memory_space=pl.ANY)
    vmem = pl.BlockSpec(memory_space=pltpu.VMEM)
    return pl.pallas_call(
        return_kernel,
        in_specs=[anywhere, anywhere, vmem, anywhere, vmem, vmem],
        out_specs=[vmem, anywhere, vmem, vmem],
        out_shape=[
            jax.ShapeDtypeStruct((count, chunks * width), bf16),
            jax.ShapeDtypeStruct((NZ, PLANE, count), f32),
            jax.ShapeDtypeStruct(old_moment.shape, f32),
            jax.ShapeDtypeStruct((wg.shape[1], BLK, BLK), bf16),
        ],
        scratch_shapes=[
            pltpu.VMEM((chunks, slots, width), bf16),
            pltpu.VMEM(sc.shape, bf16),
            pltpu.VMEM((chunks, 2, ROWS, width), bf16),
            pltpu.VMEM((chunks, NZ * count, width), f32),
            pltpu.VMEM((chunks, 2, NZ // 2, count, width), bf16),
            pltpu.VMEM((chunks, 2, NZ // 2, count, width), bf16),
            pltpu.VMEM((NZ, PLANE, count), f32),
            pltpu.VMEM(wg.shape, bf16),
            dma((chunks,)),
            dma((chunks, PLANE)),
            dma((chunks, PLANE)),
            dma((chunks, 2)),
            dma((chunks, 2)),
            dma((1,)),
            dma((1, PLANE)),
            dma((1, PLANE)),
            dma((chunks, 2, NZ // 2)),
            dma((chunks, 2, NZ // 2)),
            dma((NZ,)),
            dma((NZ,)),
            dma((NY,)),
            dma((NY,)),
            dma((2, NY // 2)),
            dma((2, NY // 2)),
        ],
        compiler_params=pltpu.CompilerParams(
            collective_id=1, has_side_effects=True, vmem_limit_bytes=56 << 20
        ),
        cost_estimate=pl.CostEstimate(
            flops=2 * slots * NZ * count * chunks * width, bytes_accessed=150 << 20, transcendentals=0
        ),
    )(pg, sc, choose, wg, own_blocks, old_moment)


def pieces(*parts):
    tiles = [a.reshape(-1, 16, BLK).astype(jnp.bfloat16) for a in parts]
    count = sum(a.shape[0] for a in tiles)
    tiles.append(jnp.zeros((NZ * PLANE - count, 16, BLK), jnp.bfloat16))
    return jnp.concatenate(tiles).reshape(NZ, PLANE, 16, BLK)


def body(tokens, out_grad, expert_ids, route_weights, blocks, layout, moments, partner):
    f32, bf16 = jnp.float32, jnp.bfloat16
    n = lax.axis_size("expert")
    n_dp = lax.axis_size("dp")
    count, width = tokens.shape
    share = BLK // n_dp
    own = lax.dynamic_slice_in_dim(blocks[0], lax.axis_index("dp") * share, share, 2)
    flat_layout = layout[0].reshape(-1)
    state = pieces(own, jnp.pad(flat_layout, (0, 16 * BLK - flat_layout.size)))
    late_state = pieces(moments[0])
    tiles = own.shape[0] * own.shape[1]

    place = Place()
    number = jnp.arange(n, dtype=jnp.int32)
    where = (place.x + number // NCORE % NX) % NX * (NZ * NCORE) + number // PLANE * NCORE + number % NCORE
    holds = partner[where]
    picks = expert_ids[None] == holds[:, None, None]
    named = jnp.any(picks, axis=2)
    before = jnp.tril(jnp.ones((count, count), bf16), -1)
    rank = dot(named.astype(bf16), before, NT)
    weight = jnp.sum(jnp.where(picks, route_weights[None].astype(f32), 0.0), axis=2)
    slot = jnp.where(named, rank + (place.z * CAP).astype(f32), -1.0)
    meta = jnp.concatenate(
        [slot.reshape(NZ, PLANE, count), weight.reshape(NZ, PLANE, count)], axis=1
    ).astype(bf16)
    xs, choose, mats, own, old_moment, lay = dispatch(
        tokens, out_grad, meta, state, late_state, partner, tiles, 8
    )
    layout_one = lay.reshape(-1)[: layout[0].size].astype(jnp.int32).reshape(layout[0].shape)
    pg, sc, wg = expert_compute(
        layout_one, place.core.reshape(1), xs, mats.reshape(blocks[0].shape), 448
    )
    token_grad, score, moment, updated = give_back(
        pg, sc[None], choose, wg, own, old_moment, count
    )
    score = jnp.sum(jnp.where(picks, score.reshape(n, count)[:, :, None], 0.0), axis=0)
    route_grad = (score / route_weights.astype(f32)).astype(bf16)
    return (
        token_grad,
        route_grad,
        updated.reshape(blocks.shape),
        moment.reshape(moments.shape),
    )


def solution(mesh):
    rows = P(("dp", "expert"), None)
    state = P("expert", None, None, None, None)
    moment = P("expert", None, None, "dp", None)
    return jax.shard_map(
        body,
        mesh=mesh,
        in_specs=(rows, rows, rows, rows, state, P("expert", None, None, None), moment, P()),
        out_specs=(rows, rows, state, moment),
        check_vma=False,
    )
```

```python
import functools

import jax
import jax.numpy as jnp
from jax import lax
from jax.experimental import pallas as pl
from jax.experimental.pallas import tpu as pltpu
from jax.sharding import PartitionSpec as P

HID = 1408
BLK = 128
CAP = 14
DECAY = 0.9
RATE = 0.01

NT = (((1,), (1,)), ((), ()))
TN = (((0,), (0,)), ((), ()))


def dot(a, b, dims=(((1,), (0,)), ((), ()))):
    return lax.dot_general(a, b, dims, preferred_element_type=jnp.float32)


def lanes(i):
    return pl.ds(pl.multiple_of(i * BLK, BLK), BLK)


def expert_kernel(lay, place_ref, x_ref, s_ref, w_ref, pg_ref, sc_ref, out_ref, wg_ref, gate, up, hg, hid, gg, ug, acc):
    nb = w_ref.shape[1]
    rows = x_ref.shape[1]
    per = x_ref.shape[2] // BLK

    def chunk(ref, i):
        return ref[i // per, :, lanes(i % per)]

    @pl.when(pl.program_id(0) == 0)
    def _():
        wg_ref[...] = jnp.zeros_like(wg_ref)

    gate[...] = jnp.zeros_like(gate)
    up[...] = jnp.zeros_like(up)
    hg[...] = jnp.zeros_like(hg)

    def first(b, carry):
        gate[:, lanes(lay[0, b, 1])] += dot(chunk(x_ref, lay[0, b, 0]), w_ref[0, b])
        up[:, lanes(lay[1, b, 1])] += dot(chunk(x_ref, lay[1, b, 0]), w_ref[1, b])
        hg[:, lanes(lay[2, b, 0])] += dot(chunk(s_ref, lay[2, b, 1]), w_ref[2, b], NT)
        return carry

    lax.fori_loop(0, nb, first, 0)

    def middle(j, score):
        g = gate[:, lanes(j)]
        u = up[:, lanes(j)]
        h = hg[:, lanes(j)]
        sig = jax.nn.sigmoid(g)
        act = g * sig
        hb = (act * u).astype(jnp.bfloat16)
        hid[:, lanes(j)] = hb
        gg[:, lanes(j)] = (h * u * sig * (1.0 + g * (1.0 - sig))).astype(jnp.bfloat16)
        ug[:, lanes(j)] = (h * act).astype(jnp.bfloat16)
        return score + hb.astype(jnp.float32) * h

    score = lax.fori_loop(0, HID // BLK, middle, jnp.zeros((rows, BLK), jnp.float32))
    total = jnp.sum(score, axis=1, keepdims=True)
    high = total.astype(jnp.bfloat16).astype(jnp.float32)
    lane = lax.broadcasted_iota(jnp.int32, (rows, BLK), 1)
    group = pl.program_id(0) * (rows // (NCORE * ROWS))
    for k in range(1, rows // (NCORE * ROWS)):
        group = group + (lax.broadcasted_iota(jnp.int32, (rows, BLK), 0) >= k * NCORE * ROWS).astype(jnp.int32)
    place = jnp.where(group == 0, 0, NX - group) * NCORE + place_ref[0]
    sc_ref[...] = jnp.where(
        lane == place, high, jnp.where(lane == place + 8, total - high, 0.0)
    ).astype(jnp.bfloat16)

    acc[...] = jnp.zeros_like(acc)

    def last(b, carry):
        r0, c0, r1, c1 = lay[0, b, 0], lay[0, b, 1], lay[1, b, 0], lay[1, b, 1]
        acc[:, lanes(r0)] += dot(gg[:, lanes(c0)], w_ref[0, b], NT)
        acc[:, lanes(r1)] += dot(ug[:, lanes(c1)], w_ref[1, b], NT)
        wg_ref[0, b] += dot(chunk(x_ref, r0), gg[:, lanes(c0)], TN)
        wg_ref[1, b] += dot(chunk(x_ref, r1), ug[:, lanes(c1)], TN)
        wg_ref[2, b] += dot(hid[:, lanes(lay[2, b, 0])], chunk(s_ref, lay[2, b, 1]), TN)
        return carry

    lax.fori_loop(0, nb, last, 0)
    for q in range(pg_ref.shape[0]):
        width = pg_ref.shape[2]
        pg_ref[q] = acc[:, q * width : (q + 1) * width].astype(jnp.bfloat16)

    @pl.when(pl.program_id(0) == pl.num_programs(0) - 1)
    def _():
        share = out_ref.shape[2]
        for y in range(out_ref.shape[0]):
            for m in range(w_ref.shape[0]):
                out_ref[y, m * nb : (m + 1) * nb] = wg_ref[m, :, y * share : (y + 1) * share, :].astype(jnp.bfloat16)


def expert_compute(layout_one, place, xs, mats, tile):
    nq, rows, width = xs.shape
    nq = nq // 2
    nm, nb = mats.shape[:2]
    row_spec = pl.BlockSpec((nq, tile, width), lambda i, lay, place: (0, i, 0))
    grad_spec = pl.BlockSpec((nq, tile, width), lambda i, lay, place: (1, i, 0))
    f32, bf16 = jnp.float32, jnp.bfloat16
    return pl.pallas_call(
        expert_kernel,
        grid_spec=pltpu.PrefetchScalarGridSpec(
            num_scalar_prefetch=2,
            grid=(rows // tile,),
            in_specs=[
                row_spec,
                grad_spec,
                pl.BlockSpec((nm, nb, BLK, BLK), lambda i, lay, place: (0, 0, 0, 0)),
            ],
            out_specs=[
                pl.BlockSpec((nq * width // 256, tile, 256), lambda i, lay, place: (0, i, 0)),
                pl.BlockSpec((tile, BLK), lambda i, lay, place: (i, 0)),
                pl.BlockSpec((NY, nm * nb, BLK // NY, BLK), lambda i, lay, place: (0, 0, 0, 0)),
            ],
            scratch_shapes=[
                pltpu.VMEM(mats.shape, f32),
                pltpu.VMEM((tile, HID), f32),
                pltpu.VMEM((tile, HID), f32),
                pltpu.VMEM((tile, HID), f32),
                pltpu.VMEM((tile, HID), bf16),
                pltpu.VMEM((tile, HID), bf16),
                pltpu.VMEM((tile, HID), bf16),
                pltpu.VMEM((tile, nq * width), f32),
            ],
        ),
        out_shape=[
            jax.ShapeDtypeStruct((nq * width // 256, rows, 256), bf16),
            jax.ShapeDtypeStruct((rows, BLK), bf16),
            jax.ShapeDtypeStruct((NY, nm * nb, BLK // NY, BLK), bf16),
        ],
        compiler_params=pltpu.CompilerParams(vmem_limit_bytes=56 << 20),
        cost_estimate=pl.CostEstimate(
            flops=8 * nb * rows * BLK * BLK * 2,
            bytes_accessed=3 * xs.size + mats.size * 6,
            transcendentals=rows * HID,
        ),
    )(layout_one, place, xs, xs, mats)


NX, NZ, NCORE, NY = 4, 8, 2, 8
PLANE = NX * NCORE
ROWS = NZ * CAP
MESH = pl.DeviceIdType.MESH


class Place:
    def __init__(self):
        me = lax.axis_index("expert")
        self.y = lax.axis_index("dp")
        self.me = me
        self.x = me // (NZ * NCORE)
        self.z = (me // NCORE) % NZ
        self.core = me % NCORE

    def along(self, dz):
        return (self.y, self.x * (NZ * NCORE) + (self.z + dz) % NZ * NCORE + self.core)

    def across(self, dx, core):
        return (self.y, (self.x + dx) % NX * (NZ * NCORE) + self.z * NCORE + core)

    def over(self, dy):
        return ((self.y + dy) % NY, self.me)

    def meet(self, with_y):
        others = [self.along(k) for k in range(1, NZ)]
        others += [self.across(dx, c) for dx in range(1, NX) for c in range(NCORE)]
        others.append(self.across(0, 1 - self.core))
        if with_y:
            others += [self.over(k) for k in range(1, NY)]
        barrier = pltpu.get_barrier_semaphore()
        for other in others:
            pl.semaphore_signal(barrier, inc=1, device_id=other, device_id_type=MESH)
        pl.semaphore_wait(barrier, len(others))


def send(src, dst, send_sem, recv_sem, device):
    return pltpu.make_async_remote_copy(
        src_ref=src,
        dst_ref=dst,
        send_sem=send_sem,
        recv_sem=recv_sem,
        device_id=device,
        device_id_type=MESH,
    )


def span(i, size):
    return pl.ds(pl.multiple_of(i * size, size), size)


class Exchange:
    def __init__(self, place, src, dst, own_sem, send_sem, recv_sem):
        self.place, self.src, self.dst = place, src, dst
        self.own_sem, self.send_sem, self.recv_sem = own_sem, send_sem, recv_sem

    def direct(self, q, dx, core):
        number = dx * NCORE + core
        landing = (NX - dx) % NX * NCORE + self.place.core
        return send(
            self.src.at[q, span(number, ROWS)],
            self.dst.at[q, span(landing, ROWS)],
            self.send_sem.at[q, number],
            self.recv_sem.at[q, landing],
            self.place.across(dx, core),
        )

    def own(self, q):
        rows = span(self.place.core, ROWS)
        return pltpu.make_async_copy(self.src.at[q, rows], self.dst.at[q, rows], self.own_sem.at[q])

    def start(self, q, steps=(2, 1, 3, 0)):
        for dx in steps:
            if dx == 0:
                self.direct(q, 0, 1 - self.place.core).start()
                self.own(q).start()
            else:
                for core in range(NCORE):
                    self.direct(q, dx, core).start()

    def arrive(self, q):
        def one(landing):
            part = self.dst.at[q, span(landing, ROWS)]
            send(part, part, self.send_sem.at[q, landing], self.recv_sem.at[q, landing], self.place.across(1, 0)).wait_recv()

        for dx in range(1, NX):
            for core in range(NCORE):
                one(dx * NCORE + core)
        one(1 - self.place.core)
        self.own(q).wait()

    def leave(self, q):
        for dx in range(1, NX):
            for core in range(NCORE):
                self.direct(q, dx, core).wait_send()
        self.direct(q, 0, 1 - self.place.core).wait_send()


class Share:
    def __init__(self, place, blocks, send_sem, recv_sem):
        self.place, self.blocks, self.send_sem, self.recv_sem = place, blocks, send_sem, recv_sem

    def hop(self, way, step, arriving):
        past = step + (1 if arriving else 0)
        source = (self.place.y + (2 * NY - past if way == 0 else past)) % NY
        n = self.blocks.shape[0]
        which = slice(0, n)
        if step == NY // 2 - 1:
            which = slice(way * (n // 2), (way + 1) * (n // 2))
        rows = self.blocks.at[which, span(source, BLK // NY)]
        device = self.place.over(1 if way == 0 else NY - 1)
        return send(rows, rows, self.send_sem.at[way, step], self.recv_sem.at[way, step], device)

    def advance(self, step):
        for way in range(2):
            if step:
                self.hop(way, step - 1, True).wait_recv()
            if step < NY // 2:
                self.hop(way, step, False).start()

    def leave(self):
        for way in range(2):
            for step in range(NY // 2):
                self.hop(way, step, False).wait_send()


class Move:
    def __init__(self, place, state, partner, held, own_sem, send_sem, recv_sem):
        self.place, self.partner, self.held = place, partner, held
        self.buffers = [state] + list(held)
        self.own_sem, self.send_sem, self.recv_sem = own_sem, send_sem, recv_sem

    def ends(self, stage):
        return self.buffers[(0, 1, 3, 4)[stage]], self.buffers[(1, 2, 4, 5)[stage]]

    def own(self, stage):
        src, dst = self.ends(stage)
        if stage % 2 == 0:
            here = self.place.z
            return pltpu.make_async_copy(src.at[here], dst.at[here], self.own_sem.at[stage])
        here = self.place.x * NCORE + self.place.core
        return pltpu.make_async_copy(src.at[:, here], dst.at[here], self.own_sem.at[stage])

    def piece(self, stage, k, core, arriving):
        place = self.place
        src, dst = self.ends(stage)
        if stage % 2 == 0:
            landing = (place.z + NZ - k) % NZ if arriving else place.z
            return send(
                src.at[(place.z + k) % NZ],
                dst.at[landing],
                self.send_sem.at[stage, k],
                self.recv_sem.at[stage, k],
                place.along(k),
            )
        other = (place.x + k) % NX * NCORE + core
        if arriving:
            return send(
                src.at[:, other],
                dst.at[other],
                self.send_sem.at[stage, k * NCORE + core],
                self.recv_sem.at[stage, k * NCORE + core],
                place.across(k, core),
            )
        return send(
            src.at[:, other],
            dst.at[place.x * NCORE + place.core],
            self.send_sem.at[stage, k * NCORE + core],
            self.recv_sem.at[stage, (NX - k) % NX * NCORE + place.core],
            place.across(k, core),
        )

    def pieces(self, stage, arriving):
        if stage % 2 == 0:
            return [self.piece(stage, k, 0, arriving) for k in range(1, NZ)]
        rest = [self.piece(stage, k, c, arriving) for k in range(1, NX) for c in range(NCORE)]
        return rest + [self.piece(stage, 0, 1 - self.place.core, arriving)]

    def start(self, stage):
        for copy in self.pieces(stage, False):
            copy.start()
        self.own(stage).start()

    def arrive(self, stage):
        for copy in self.pieces(stage, True):
            copy.wait_recv()
        self.own(stage).wait()

    def leave(self):
        for stage in range(4):
            for copy in self.pieces(stage, False):
                copy.wait_send()

    def order(self):
        def one(slot, carry):
            z, j = slot // PLANE, slot % PLANE
            expert = self.partner[j // NCORE * (NZ * NCORE) + z * NCORE + j % NCORE]
            j_from = expert // (NZ * NCORE) * NCORE + expert % NCORE
            self.held[2][z, j] = self.held[1][j_from, expert // NCORE % NZ]
            return carry

        lax.fori_loop(0, NZ * PLANE, one, 0)

    def tile(self, t):
        return self.held[4][t % PLANE, t // PLANE]


def dispatch_kernel(
    tok, og, meta, state, partner, xs, chosen, blocks, own_rows, lay, ring, picked, choose, turned, notes,
    held_0, held_1, held_2, held_3, held_4,
    own_sem, notes_send, notes_recv, ring_send, ring_recv, out_own, out_send, out_recv, keep_sem,
    move_own, move_send, move_recv, share_send, share_recv,
):
    count = tok.shape[0]
    chunks, _, width = ring.shape
    half = chunks // 2
    place = Place()
    z = place.z
    out = Exchange(place, picked, xs, out_own, out_send, out_recv)
    move = Move(place, state, partner, (held_0, held_1, held_2, held_3, held_4), move_own, move_send, move_recv)
    share = Share(place, blocks, share_send, share_recv)

    def own_copy(q):
        src = tok if q < half else og
        return pltpu.make_async_copy(
            src.at[:, (q % half) * width : (q % half + 1) * width],
            ring.at[q, span(z, count)],
            own_sem.at[q],
        )

    for q in range(chunks):
        own_copy(q).start()
    own_notes = pltpu.make_async_copy(meta.at[z], notes.at[z], keep_sem.at[1])
    own_notes.start()
    place.meet(True)

    def note(k, source):
        return send(
            meta.at[(z + k) % NZ], notes.at[source], notes_send.at[k], notes_recv.at[k], place.along(k)
        )

    def hop(q, way, step, arriving):
        rows = count
        if way == 0:
            source = (z + 2 * NZ - step - (1 if arriving else 0)) % NZ
        else:
            source = (z + step + (1 if arriving else 0)) % NZ
        start = source * count
        if step == NZ // 2 - 1:
            rows = count // 2
            start = start + way * rows
        block = ring.at[q, pl.ds(pl.multiple_of(start, rows), rows)]
        return send(
            block,
            block,
            ring_send.at[q, way, step],
            ring_recv.at[q, way, step],
            place.along(1 if way == 0 else NZ - 1),
        )

    for k in range(1, NZ):
        note(k, z).start()
    for q in range(chunks):
        own_copy(q).wait()
    own_notes.wait()
    for way in range(2):
        hop(0, way, 0, False).start()
    move.start(0)
    for way in range(2):
        hop(1, way, 0, False).start()

    def unpack():
        n = blocks.shape[0]

        def one(b, carry):
            rows = move.tile(b)
            own_rows[b] = rows
            blocks[b, span(place.y, BLK // NY), :] = rows
            return carry

        lax.fori_loop(0, n, one, 0)
        lay[...] = move.tile(n)

    def keep():
        return pltpu.make_async_copy(turned, chosen, keep_sem.at[0])

    def build():
        for k in range(1, NZ):
            note(k, (z + NZ - k) % NZ).wait_recv()
        row = lax.broadcasted_iota(jnp.int32, (ROWS, count), 0).astype(jnp.float32)

        def fill(source, carry):
            both = notes[source].astype(jnp.float32)
            for other in range(PLANE):
                hit = row == both[other : other + 1, :]
                rows = slice(other * ROWS, (other + 1) * ROWS)
                scale = both[PLANE + other : PLANE + other + 1, :]
                choose[0, rows, span(source, count)] = jnp.where(hit, 1.0, 0.0).astype(jnp.bfloat16)
                choose[1, rows, span(source, count)] = jnp.where(hit, scale, 0.0).astype(jnp.bfloat16)
            return carry

        lax.fori_loop(0, NZ, fill, 0)

    def turn():
        def one(source, carry):
            block = choose[0, :, span(source, count)].astype(jnp.float32)
            turned[span(source, count), :] = block.T.astype(jnp.bfloat16)
            return carry

        lax.fori_loop(0, NZ, one, 0)
        keep().start()

    def step(i, carry):
        for s in range(NZ // 2):
            q = i - s if s else i + 2

            @pl.when((q >= 0) & (q < chunks))
            def _():
                for way in range(2):
                    if s:
                        hop(q, way, s - 1, True).wait_recv()
                    hop(q, way, s, False).start()

        pl.when(i == 1)(build)
        pl.when(i == NZ // 2 + 3)(turn)

        q = i - NZ // 2

        @pl.when((q >= 0) & (q < chunks))
        def _():
            for way in range(2):
                hop(q, way, NZ // 2 - 1, True).wait_recv()
            for h in (1, 0):
                rows = slice(h * (PLANE // 2) * ROWS, (h + 1) * (PLANE // 2) * ROWS)
                picked[q, rows, :] = dot(choose[q // half, rows, :], ring[q]).astype(jnp.bfloat16)
                out.start(q, (2, 3) if h else (1, 0))

        @pl.when(i == 3)
        def _():
            move.arrive(0)
            move.start(1)

        @pl.when(i == 5)
        def _():
            move.arrive(1)
            move.order()
            move.start(2)

        @pl.when(i == 8)
        def _():
            move.arrive(2)
            move.start(3)

        @pl.when(i == 10)
        def _():
            move.arrive(3)
            unpack()
            share.advance(0)

        for s in range(1, NY // 2 + 1):

            @pl.when(i == 10 + s)
            def _():
                share.advance(s)

        return carry

    lax.fori_loop(0, chunks + NZ // 2, step, 0)

    def finish(q, carry):
        for way in range(2):
            for s in range(NZ // 2):
                hop(q, way, s, False).wait_send()
        out.leave(q)
        out.arrive(q)
        return carry

    lax.fori_loop(0, chunks, finish, 0)
    for k in range(1, NZ):
        note(k, z).wait_send()
    keep().wait()
    move.leave()
    share.leave()


def dispatch(tokens, grads, meta, state, partner, tiles, chunks):
    count, features = tokens.shape
    width = 2 * features // chunks
    bf16 = jnp.bfloat16
    slots = PLANE * ROWS
    dma = pltpu.SemaphoreType.DMA
    anywhere = pl.BlockSpec(memory_space=pl.ANY)
    return pl.pallas_call(
        dispatch_kernel,
        in_specs=[anywhere] * 4 + [pl.BlockSpec(memory_space=pltpu.SMEM)],
        out_specs=[anywhere, anywhere] + [pl.BlockSpec(memory_space=pltpu.VMEM)] * 3,
        out_shape=[
            jax.ShapeDtypeStruct((chunks, slots, width), bf16),
            jax.ShapeDtypeStruct((NZ * count, slots), bf16),
            jax.ShapeDtypeStruct((tiles, BLK, BLK), bf16),
            jax.ShapeDtypeStruct((tiles, BLK // NY, BLK), bf16),
            jax.ShapeDtypeStruct((BLK // NY, BLK), bf16),
        ],
        scratch_shapes=[
            pltpu.VMEM((chunks, NZ * count, width), bf16),
            pltpu.VMEM((chunks, slots, width), bf16),
            pltpu.VMEM((2, slots, NZ * count), bf16),
            pltpu.VMEM((NZ * count, slots), bf16),
            pltpu.VMEM(meta.shape, bf16),
            *[pltpu.VMEM(state.shape, bf16)] * 5,
            dma((chunks,)),
            dma((NZ,)),
            dma((NZ,)),
            dma((chunks, 2, NZ // 2)),
            dma((chunks, 2, NZ // 2)),
            dma((chunks,)),
            dma((chunks, PLANE)),
            dma((chunks, PLANE)),
            dma((2,)),
            dma((4,)),
            dma((4, NZ)),
            dma((4, NZ)),
            dma((2, NY // 2)),
            dma((2, NY // 2)),
        ],
        compiler_params=pltpu.CompilerParams(
            collective_id=0, has_side_effects=True, vmem_limit_bytes=56 << 20
        ),
        cost_estimate=pl.CostEstimate(
            flops=2 * slots * NZ * count * 2 * features, bytes_accessed=300 << 20, transcendentals=0
        ),
    )(tokens, grads, meta, state, partner)


def return_kernel(
    pg, sc, choose, wg, own_blocks, late_state, partner, tg, score, moment, blocks,
    back, marks, part, leaving, landed, sums, grads, held_0, held_1, held_2, held_3, held_4,
    x_own, x_send, x_recv, mark_own, mark_send, mark_recv,
    z_send, z_recv, sum_send, sum_recv, y_send, y_recv, share_send, share_recv,
    move_own, move_send, move_recv,
):
    chunks, slots, width = pg.shape
    count = tg.shape[0]
    last = NZ // 2 - 1
    place = Place()
    z, y = place.z, place.y
    cross = Exchange(place, pg, back, x_own, x_send, x_recv)
    mark = Exchange(place, sc, marks, mark_own, mark_send, mark_recv)

    move = Move(place, late_state, partner, (held_0, held_1, held_2, held_3, held_4), move_own, move_send, move_recv)

    own_grads = pltpu.make_async_copy(wg.at[y], grads.at[y], y_send.at[0])
    own_grads.start()
    place.meet(True)
    cross.start(0)
    move.start(0)

    def grad(k, landing):
        return send(wg.at[(y + k) % NY], grads.at[landing], y_send.at[k], y_recv.at[k], place.over(k))

    for k in range(1, NY):
        grad(k, y).start()
    cross.start(1)
    cross.start(2)
    mark.start(0)

    share = Share(place, blocks, share_send, share_recv)

    def update():
        move.arrive(3)
        for k in range(1, NY):
            grad(k, (y + NY - k) % NY).wait_recv()
        own_grads.wait()

        def one(b, carry):
            total = DECAY * move.tile(b).astype(jnp.float32)
            for source in range(NY):
                total = total + grads[source, b].astype(jnp.float32)
            moment[b] = total
            fresh = own_blocks[b].astype(jnp.float32) - RATE * total
            blocks[b, span(y, BLK // NY), :] = fresh.astype(jnp.bfloat16)
            return carry

        lax.fori_loop(0, blocks.shape[0], one, 0)
        share.advance(0)

    def hop(q, way, step):
        rows = slice(0, count)
        if step == 0:
            rows = slice(way * (count // 2), (way + 1) * (count // 2))
        return send(
            leaving.at[q, way, step, rows],
            landed.at[q, way, step, rows],
            z_send.at[q, way, step],
            z_recv.at[q, way, step],
            place.along(1 if way == 0 else NZ - 1),
        )

    def target(way, step):
        if way == 0:
            return (z + NZ // 2 - step) % NZ
        return (z + NZ // 2 + step) % NZ

    def own_sum():
        return pltpu.make_async_copy(sums.at[z], score.at[z], sum_send.at[0])

    def summed(k, landing):
        return send(sums.at[(z + k) % NZ], score.at[landing], sum_send.at[k], sum_recv.at[k], place.along(k))

    def step(i, carry):
        @pl.when(i < chunks)
        def _():
            q = i
            cross.arrive(q)

            def add(t, carry):
                cols = span(t, 2 * count)
                part[q, cols, :] = dot(choose[cols, :], back[q])
                return carry

            lax.fori_loop(0, NZ // 2, add, 0)
            for way in range(2):
                size = count // 2
                start = target(way, 0) * count + way * size
                rows = pl.ds(pl.multiple_of(start, size), size)
                leaving[q, way, 0, way * size : (way + 1) * size, :] = part[q, rows, :].astype(jnp.bfloat16)
                hop(q, way, 0).start()

        for s in range(1, NZ // 2):
            q = i - s

            @pl.when((q >= 0) & (q < chunks))
            def _():
                for way in range(2):
                    hop(q, way, s - 1).wait_recv()
                    mine = part[q, span(target(way, s), count), :]
                    if s == 1:
                        size = count // 2
                        near = slice(way * size, (way + 1) * size)
                        far = slice((1 - way) * size, (2 - way) * size)
                        more = landed[q, way, 0, near, :].astype(jnp.float32)
                        leaving[q, way, 1, near, :] = (mine[near] + more).astype(jnp.bfloat16)
                        leaving[q, way, 1, far, :] = mine[far].astype(jnp.bfloat16)
                    else:
                        more = landed[q, way, s - 1].astype(jnp.float32)
                        leaving[q, way, s] = (mine + more).astype(jnp.bfloat16)
                    hop(q, way, s).start()

        q = i - NZ // 2

        @pl.when(q >= 0)
        def _():
            total = part[q, span(z, count), :]
            for way in range(2):
                hop(q, way, last).wait_recv()
                total = total + landed[q, way, last].astype(jnp.float32)
            tg[:, pl.ds(pl.multiple_of(q * width, width), width)] = total.astype(jnp.bfloat16)

        @pl.when(i + 3 < chunks)
        def _():
            cross.start(i + 3)

        @pl.when(i == 1)
        def _():
            move.arrive(0)
            move.start(1)

        @pl.when(i == 3)
        def _():
            move.arrive(1)
            move.order()
            move.start(2)

        @pl.when(i == 5)
        def _():
            move.arrive(2)
            move.start(3)

        pl.when(i == 7)(update)
        for s in range(1, NY // 2 + 1):

            @pl.when(i == 7 + s)
            def _():
                share.advance(s)

        @pl.when(i == chunks - 1)
        def _():
            mark.arrive(0)
            spread = dot(marks[0], choose[...], (((0,), (1,)), ((), ())))
            both = spread[:PLANE] + spread[PLANE : 2 * PLANE]
            for source in range(NZ):
                sums[source] = both[:, source * count : (source + 1) * count]
            own_sum().start()
            for k in range(1, NZ):
                summed(k, z).start()

        return carry

    lax.fori_loop(0, chunks + NZ // 2, step, 0)

    def finish(q, carry):
        cross.leave(q)
        for way in range(2):
            for s in range(NZ // 2):
                hop(q, way, s).wait_send()
        return carry

    lax.fori_loop(0, chunks, finish, 0)
    mark.leave(0)
    own_sum().wait()
    for k in range(1, NZ):
        summed(k, z).wait_send()
        summed(k, (z + NZ - k) % NZ).wait_recv()
    for k in range(1, NY):
        grad(k, y).wait_send()
    share.leave()
    move.leave()


def give_back(pg, sc, choose, wg, own_blocks, late_state, partner, count):
    chunks, slots, width = pg.shape
    f32, bf16 = jnp.float32, jnp.bfloat16
    dma = pltpu.SemaphoreType.DMA
    anywhere = pl.BlockSpec(memory_space=pl.ANY)
    vmem = pl.BlockSpec(memory_space=pltpu.VMEM)
    return pl.pallas_call(
        return_kernel,
        in_specs=[anywhere, anywhere, vmem, anywhere, vmem, anywhere, pl.BlockSpec(memory_space=pltpu.SMEM)],
        out_specs=[vmem, anywhere, vmem, vmem],
        out_shape=[
            jax.ShapeDtypeStruct((count, chunks * width), bf16),
            jax.ShapeDtypeStruct((NZ, PLANE, count), f32),
            jax.ShapeDtypeStruct(own_blocks.shape, f32),
            jax.ShapeDtypeStruct((wg.shape[1], BLK, BLK), bf16),
        ],
        scratch_shapes=[
            pltpu.VMEM((chunks, slots, width), bf16),
            pltpu.VMEM(sc.shape, bf16),
            pltpu.VMEM((chunks, NZ * count, width), f32),
            pltpu.VMEM((chunks, 2, NZ // 2, count, width), bf16),
            pltpu.VMEM((chunks, 2, NZ // 2, count, width), bf16),
            pltpu.VMEM((NZ, PLANE, count), f32),
            pltpu.VMEM(wg.shape, bf16),
            *[pltpu.VMEM(late_state.shape, bf16)] * 5,
            dma((chunks,)),
            dma((chunks, PLANE)),
            dma((chunks, PLANE)),
            dma((1,)),
            dma((1, PLANE)),
            dma((1, PLANE)),
            dma((chunks, 2, NZ // 2)),
            dma((chunks, 2, NZ // 2)),
            dma((NZ,)),
            dma((NZ,)),
            dma((NY,)),
            dma((NY,)),
            dma((2, NY // 2)),
            dma((2, NY // 2)),
            dma((4,)),
            dma((4, NZ)),
            dma((4, NZ)),
        ],
        compiler_params=pltpu.CompilerParams(
            collective_id=1, has_side_effects=True, vmem_limit_bytes=56 << 20
        ),
        cost_estimate=pl.CostEstimate(
            flops=2 * slots * NZ * count * chunks * width, bytes_accessed=150 << 20, transcendentals=0
        ),
    )(pg, sc, choose, wg, own_blocks, late_state, partner)


def pieces(*parts):
    tiles = [a.reshape(-1, 16, BLK).astype(jnp.bfloat16) for a in parts]
    count = sum(a.shape[0] for a in tiles)
    tiles.append(jnp.zeros((NZ * PLANE - count, 16, BLK), jnp.bfloat16))
    return jnp.concatenate(tiles).reshape(NZ, PLANE, 16, BLK)


def body(tokens, out_grad, expert_ids, route_weights, blocks, layout, moments, partner):
    f32, bf16 = jnp.float32, jnp.bfloat16
    n = lax.axis_size("expert")
    n_dp = lax.axis_size("dp")
    count, width = tokens.shape
    share = BLK // n_dp
    own = lax.dynamic_slice_in_dim(blocks[0], lax.axis_index("dp") * share, share, 2)
    flat_layout = layout[0].reshape(-1)
    state = pieces(own, jnp.pad(flat_layout, (0, 16 * BLK - flat_layout.size)))
    late_state = pieces(moments[0])
    tiles = own.shape[0] * own.shape[1]

    place = Place()
    number = jnp.arange(n, dtype=jnp.int32)
    where = (place.x + number // NCORE % NX) % NX * (NZ * NCORE) + number // PLANE * NCORE + number % NCORE
    holds = partner[where]
    picks = expert_ids[None] == holds[:, None, None]
    named = jnp.any(picks, axis=2)
    before = jnp.tril(jnp.ones((count, count), bf16), -1)
    rank = dot(named.astype(bf16), before, NT)
    weight = jnp.sum(jnp.where(picks, route_weights[None].astype(f32), 0.0), axis=2)
    slot = jnp.where(named, rank + (place.z * CAP).astype(f32), -1.0)
    meta = jnp.concatenate(
        [slot.reshape(NZ, PLANE, count), weight.reshape(NZ, PLANE, count)], axis=1
    ).astype(bf16)
    xs, choose, mats, own, lay = dispatch(
        tokens, out_grad, meta, state, partner, tiles, 16
    )
    layout_one = lay.reshape(-1)[: layout[0].size].astype(jnp.int32).reshape(layout[0].shape)
    pg, sc, wg = expert_compute(
        layout_one, place.core.reshape(1), xs, mats.reshape(blocks[0].shape), 448
    )
    token_grad, score, moment, updated = give_back(
        pg, sc[None], choose, wg, own, late_state, partner, count
    )
    score = jnp.sum(jnp.where(picks, score.reshape(n, count)[:, :, None], 0.0), axis=0)
    route_grad = (score / route_weights.astype(f32)).astype(bf16)
    return (
        token_grad,
        route_grad,
        updated.reshape(blocks.shape),
        moment.reshape(moments.shape),
    )


def solution(mesh):
    rows = P(("dp", "expert"), None)
    state = P("expert", None, None, None, None)
    moment = P("expert", None, None, "dp", None)
    return jax.shard_map(
        body,
        mesh=mesh,
        in_specs=(rows, rows, rows, rows, state, P("expert", None, None, None), moment, P()),
        out_specs=(rows, rows, state, moment),
        check_vma=False,
    )
```
